512 devices in a mesh: seq: 64 (over y, z_lo, x), blk: 8 (over z_hi, core).
Axes of the slice: x: 4, y: 8, z: 8 (z_hi: 4, z_lo: 2; z = z_hi * 2 + z_lo), core: 2. Of those that a mesh axis runs over, the one named last changes fastest.
Arguments:
- base_ids: int32 [32768], P('seq'), may hold values from 0 to 3
- span_start: int32 [4096], replicated, may hold values from 0 to 32760
- span_length: int32 [4096], replicated, may hold values from 1 to 8
- embedding: bfloat16 [5, 2048], P(None, 'blk'), may hold values from -6 to 6
- conv_kernel: bfloat16 [2, 9, 2048], P(None, None, 'blk'), may hold values from -2 to 2
- mix_weight: bfloat16 [2, 2048, 2048], P(None, 'blk'), may hold values from -0.125 to 0.125
- saved_input: bfloat16 [32768, 2048], P('seq', 'blk'), may hold values from -6 to 6
- cotangent: bfloat16 [32768, 2048], P('seq', 'blk'), may hold values from -6 to 6
Outputs:
- input_grad: bfloat16 [32768, 2048], P('seq', 'blk')
- weight_grad: float32 [2, 2048, 2048], P(None, ('blk', 'seq'))
- kernel_grad: float32 [2, 9, 2048], P(None, None, 'blk')
- embed_grad: float32 [5, 2048], P(None, 'blk')
The draws below stay inside these ranges and needn't reach their ends.
Inputs may be any that keep to these rules, and one draw needn't show every extreme that they name: Span j masks the positions span_start[j] to span_start[j] + span_length[j] - 1, all inside the window; spans may share positions or touch.
All inputs are finite; a program needn't handle non-finite values.
Results may differ from the reference program's by a relative error of at most 0.007.
Values may be sent and summed in bfloat16 or wider, within the bound.
No kernel may reach another device: no remote copies, remote signals or barrier semaphores. Data moves between devices by JAX's collectives and lax.ppermute only.
A program may use at most 64 MiB of HBM per device.

```python
import math
import jax
import jax.numpy as jnp
from jax import lax

D = 2048
KSIZE = 9
BASE_DILATION = 4
NB = 2
VOCAB = 5
MAXLEN = 8
TOKENS = 32768
SPANS = 4096


def set_ends(values, rng, low, largest):
    longest = values.shape.index(max(values.shape))
    spots = []
    for shift in (0, 1):
        where = [jax.random.randint(jax.random.fold_in(rng, axis), (), 0, length) for axis, length in enumerate(values.shape)]
        where[longest] = (where[longest] + shift) % values.shape[longest]
        spots.append(tuple(where))
    return values.at[spots[0]].set(low).at[spots[1]].set(largest)


def level_of(key, dims, pieces, least, top_value):
    gain, own = 1.0, jax.random.fold_in(key, 6)
    for dim, blocks in pieces:
        draws = jnp.exp(jax.random.uniform(jax.random.fold_in(own, dim), (blocks,), jnp.float32, least / len(pieces), top_value / len(pieces)))
        gain = gain * jnp.repeat(draws, dims[dim] // blocks).reshape([-1 if axis == dim else 1 for axis in range(len(dims))])
    return gain


def noise(stream_key, dims, width, reach, pieces=(), kind=jnp.bfloat16):
    values = width * jax.random.normal(stream_key, dims, jnp.float32)
    if pieces:
        values = values * level_of(stream_key, dims, pieces, -0.22, 0.18)
    return jnp.clip(values, -reach, reach).astype(kind)


def setup_inputs(seed: int = 0) -> dict:
    key_of = jax.random.split(jax.random.key(seed), 9)
    base_ids = set_ends(jax.random.randint(key_of[0], (TOKENS,), 0, 4), jax.random.fold_in(key_of[0], 1), 0, 3).astype(jnp.int32)
    span_start = set_ends(jax.random.randint(key_of[1], (SPANS,), 0, TOKENS - MAXLEN + 1), jax.random.fold_in(key_of[1], 1), 0, TOKENS - MAXLEN).astype(jnp.int32)
    span_length = set_ends(jax.random.randint(key_of[2], (SPANS,), 1, MAXLEN + 1), jax.random.fold_in(key_of[2], 1), 1, MAXLEN).astype(jnp.int32)
    embedding = noise(key_of[3], (VOCAB, D), 1.0, 6.0, ((1, 8),))
    conv_kernel = noise(key_of[4], (NB, KSIZE, D), KSIZE ** -0.5, 2.0, ((2, 8),))
    mix_weight = noise(key_of[5], (NB, D, D), D ** -0.5, 0.125, ((1, 8),))
    saved_input = noise(key_of[6], (TOKENS, D), 1.0, 6.0, ((0, 64), (1, 8)))
    cotangent = noise(key_of[7], (TOKENS, D), 1.0, 6.0, ((0, 64), (1, 8)))
    return {"base_ids": base_ids, "span_start": span_start, "span_length": span_length, "embedding": embedding, "conv_kernel": conv_kernel, "mix_weight": mix_weight, "saved_input": saved_input, "cotangent": cotangent}


mask_token = 4
gelu_scale = 0.7978845608028654
gelu_cubic = 0.044715

def gelu_pair(pre_act):
    inner_arg = gelu_scale * (pre_act + gelu_cubic * pre_act * pre_act * pre_act)
    tangent = jnp.tanh(inner_arg)
    activation = 0.5 * pre_act * (1.0 + tangent)
    derivative = 0.5 * (1.0 + tangent) + 0.5 * pre_act * (1.0 - tangent * tangent) * gelu_scale * (1.0 + 3.0 * gelu_cubic * pre_act * pre_act)
    return (activation, derivative)

def tap_sum(padded, kernel, tap_spacing, row_count, flipped):
    tap_count = kernel.shape[0]
    running = jnp.zeros((row_count, padded.shape[1]), jnp.float32)
    for tap_index in range(tap_count):
        source = tap_count - 1 - tap_index if flipped else tap_index
        window = padded[source * tap_spacing:source * tap_spacing + row_count].astype(jnp.float32)
        running = running + kernel[tap_index].astype(jnp.float32) * window
    return running

def tap_products(grad_pre, padded, tap_spacing, tap_count):
    row_count = grad_pre.shape[0]
    grad_wide = grad_pre.astype(jnp.float32)
    output_rows = []
    for tap_index in range(tap_count):
        window = padded[tap_index * tap_spacing:tap_index * tap_spacing + row_count].astype(jnp.float32)
        output_rows.append(lax.optimization_barrier(jnp.sum(grad_wide * window, axis=0)))
    return jnp.stack(output_rows)

def reference(base_ids, span_start, span_length, embedding, conv_kernel, mix_weight, saved_input, cotangent):
    span_marks = jnp.zeros((TOKENS + 1,), jnp.int32)
    span_marks = span_marks.at[span_start].add(1).at[span_start + span_length].add(-1)
    covered = jnp.cumsum(span_marks)[:TOKENS] > 0
    masked_ids = jnp.where(covered, mask_token, base_ids).astype(jnp.int32)
    block_inputs = [embedding[masked_ids], saved_input]
    grad_scale = 1.0 / math.sqrt(TOKENS)
    upstream = jnp.where(covered[:, None], cotangent, jnp.zeros_like(cotangent))
    weight_list = [None] * NB
    kernel_list = [None] * NB
    for block_number in range(NB - 1, -1, -1):
        tap_spacing = BASE_DILATION * 2 ** block_number
        reach_rows = KSIZE // 2 * tap_spacing
        padded_in = jnp.pad(block_inputs[block_number], ((reach_rows, reach_rows), (0, 0)))
        pre_act = tap_sum(padded_in, conv_kernel[block_number], tap_spacing, TOKENS, False)
        activation, derivative = gelu_pair(pre_act)
        act_half = activation.astype(jnp.bfloat16)
        grad_act = jnp.dot(upstream, mix_weight[block_number].T, preferred_element_type=jnp.float32)
        grad_pre = (grad_act * derivative).astype(jnp.bfloat16)
        weight_list[block_number] = jnp.dot(act_half.T, upstream, preferred_element_type=jnp.float32) * grad_scale
        kernel_list[block_number] = tap_products(grad_pre, padded_in, tap_spacing, KSIZE) * grad_scale
        padded_grad = jnp.pad(grad_pre, ((reach_rows, reach_rows), (0, 0)))
        upstream = (upstream.astype(jnp.float32) + tap_sum(padded_grad, conv_kernel[block_number], tap_spacing, TOKENS, True)).astype(jnp.bfloat16)
    one_hot = (jnp.arange(VOCAB, dtype=jnp.int32)[:, None] == masked_ids[None, :]).astype(jnp.bfloat16)
    embed_grad = jnp.dot(one_hot, upstream, preferred_element_type=jnp.float32) * grad_scale
    return (upstream, jnp.stack(weight_list), jnp.stack(kernel_list), embed_grad)
```

```python
import math

import jax
import jax.numpy as jnp
from jax import lax
from jax.sharding import Mesh, PartitionSpec as P

BASE_DILATION = 4

SEQ = ("y", "zl", "x")
BLK = ("zh", "core")
NEAR = ("zl", "x")
FAR = ("y",)

mask_token = 4
gelu_scale = 0.7978845608028654
gelu_cubic = 0.044715


def extended(cells, sides, width):
    for axis, dim in sides:
        count = lax.axis_size(axis)
        ends = count - 1
        head = lax.slice_in_dim(cells, 0, width, axis=dim)
        tail = lax.slice_in_dim(cells, cells.shape[dim] - width, cells.shape[dim], axis=dim)
        cells = jnp.concatenate(
            [
                lax.ppermute(tail, axis, [(i, (i + 1) % count) for i in range(ends)]),
                cells,
                lax.ppermute(head, axis, [((i + 1) % count, i) for i in range(ends)]),
            ],
            axis=dim,
        )
    return cells


def gelu_pair(pre_act):
    inner_arg = gelu_scale * (pre_act + gelu_cubic * pre_act * pre_act * pre_act)
    tangent = jnp.tanh(inner_arg)
    activation = 0.5 * pre_act * (1.0 + tangent)
    derivative = 0.5 * (1.0 + tangent) + 0.5 * pre_act * (1.0 - tangent * tangent) * gelu_scale * (
        1.0 + 3.0 * gelu_cubic * pre_act * pre_act
    )
    return (activation, derivative)


def tap_sum(padded, kernel, tap_spacing, row_count, flipped):
    tap_count = kernel.shape[0]
    running = jnp.zeros((row_count, padded.shape[1]), jnp.float32)
    for tap_index in range(tap_count):
        source = tap_count - 1 - tap_index if flipped else tap_index
        window = padded[source * tap_spacing : source * tap_spacing + row_count].astype(jnp.float32)
        running = running + kernel[tap_index].astype(jnp.float32) * window
    return running


def tap_products(grad_pre, padded, tap_spacing, tap_count):
    row_count = grad_pre.shape[0]
    grad_wide = grad_pre.astype(jnp.float32)
    output_rows = []
    for tap_index in range(tap_count):
        window = padded[tap_index * tap_spacing : tap_index * tap_spacing + row_count].astype(
            jnp.float32
        )
        output_rows.append(jnp.sum(grad_wide * window, axis=0))
    return jnp.stack(output_rows)


def covered_at(positions, span_start, span_length):
    span_end = span_start + span_length
    within = (positions[:, None] >= span_start[None, :]) & (positions[:, None] < span_end[None, :])
    return jnp.any(within, axis=1)


def lookup(hot_rows, table_rows):
    return jnp.einsum("vt,vc->tc", hot_rows, table_rows, preferred_element_type=jnp.float32).astype(
        jnp.bfloat16
    )


def scatter_sum(part):
    near, far = lax.axis_size(NEAR), lax.axis_size(FAR)
    rows, width = part.shape
    own = rows // (near * far)
    pieces = part.astype(jnp.bfloat16).reshape(far, near, own, width)
    pieces = pieces.transpose(1, 0, 2, 3).reshape(near, far * own, width)
    pieces = lax.all_to_all(pieces, NEAR, 0, 0)
    half = jnp.sum(pieces.astype(jnp.float32), axis=0).astype(jnp.bfloat16)
    pieces = lax.all_to_all(half.reshape(far, own, width), FAR, 0, 0)
    return jnp.sum(pieces.astype(jnp.float32), axis=0)


def whole_sum(part):
    for axes in (NEAR, FAR):
        copies = jnp.broadcast_to(part[None], (lax.axis_size(axes),) + part.shape)
        part = jnp.sum(lax.all_to_all(copies, axes, 0, 0), axis=0)
    return part


def on_device(
    base_ids, span_start, span_length, embedding, conv_kernel, mix_weight, saved_input, cotangent
):
    row_count = saved_input.shape[0]
    block_count = conv_kernel.shape[0]
    tap_count = conv_kernel.shape[1]
    taps_per_side = tap_count // 2
    vocab_rows = embedding.shape[0]
    total_rows = row_count * lax.axis_size(SEQ)
    grad_scale = 1.0 / math.sqrt(total_rows)
    first_row = lax.axis_index(SEQ) * row_count
    positions = first_row + jnp.arange(row_count, dtype=jnp.int32)
    covered = covered_at(positions, span_start, span_length)
    masked_ids = jnp.where(covered, mask_token, base_ids)
    vocab_ids = jnp.arange(vocab_rows, dtype=jnp.int32)
    one_hot = (vocab_ids[:, None] == masked_ids[None, :]).astype(jnp.bfloat16)
    initial_reach = taps_per_side * BASE_DILATION
    first_input = lookup(one_hot, embedding)
    first_padded = extended(first_input, ((SEQ, 0),), initial_reach)
    upstream = jnp.where(covered[:, None], cotangent, jnp.zeros_like(cotangent))
    weight_parts = [None] * block_count
    kernel_parts = [None] * block_count
    for block_number in range(block_count - 1, -1, -1):
        tap_spacing = BASE_DILATION * 2**block_number
        reach_rows = taps_per_side * tap_spacing
        if block_number == 0:
            padded_in = first_padded
        else:
            padded_in = extended(saved_input, ((SEQ, 0),), reach_rows)
        kernel = conv_kernel[block_number]
        weight_rows = mix_weight[block_number]
        pre_act = tap_sum(padded_in, kernel, tap_spacing, row_count, False)
        activation, derivative = gelu_pair(pre_act)
        act_half = activation.astype(jnp.bfloat16)
        column_piece = lax.all_gather(upstream, BLK, axis=1, tiled=True)
        grad_held = lax.dot_general(
            column_piece, weight_rows, (((1,), (1,)), ((), ())), preferred_element_type=jnp.float32
        )
        block_part = lax.dot_general(
            act_half, column_piece, (((0,), (0,)), ((), ())), preferred_element_type=jnp.float32
        )
        grad_pre = (grad_held * derivative).astype(jnp.bfloat16)
        kernel_parts[block_number] = (
            tap_products(grad_pre, padded_in, tap_spacing, tap_count) * grad_scale
        )
        padded_grad = extended(grad_pre, ((SEQ, 0),), reach_rows)
        upstream = (
            upstream.astype(jnp.float32)
            + tap_sum(padded_grad, kernel, tap_spacing, row_count, True)
        ).astype(jnp.bfloat16)
        weight_parts[block_number] = scatter_sum(block_part) * grad_scale
    weight_grad = jnp.stack(weight_parts)
    embed_part = jnp.dot(one_hot, upstream, preferred_element_type=jnp.float32) * grad_scale
    small = jnp.concatenate(kernel_parts + [embed_part, jnp.zeros((1, embed_part.shape[1]))])
    small = whole_sum(small)
    split = block_count * tap_count
    kernel_grad = small[:split].reshape(block_count, tap_count, -1)
    embed_grad = small[split : split + vocab_rows]
    return (upstream, weight_grad, kernel_grad, embed_grad)


def solution(mesh):
    fine = Mesh(mesh.devices.reshape(8, 2, 4, 4, 2), SEQ + BLK)
    placed = (
        P(SEQ),
        P(),
        P(),
        P(None, BLK),
        P(None, None, BLK),
        P(None, BLK, None),
        P(SEQ, BLK),
        P(SEQ, BLK),
    )
    return jax.shard_map(
        on_device,
        mesh=fine,
        in_specs=placed,
        out_specs=(
            P(SEQ, BLK),
            P(None, BLK + SEQ, None),
            P(None, None, BLK),
            P(None, BLK),
        ),
        check_vma=False,
    )
```

```python
import functools
import math

import jax
import jax.numpy as jnp
from jax import lax
from jax.experimental import pallas as pl
from jax.experimental.pallas import tpu as pltpu
from jax.sharding import Mesh, PartitionSpec as P

BASE_DILATION = 4

SEQ = ("y", "zl", "x")
BLK = ("zh", "core")
NEAR = ("zl", "x")
FAR = ("y",)

mask_token = 4
gelu_scale = 0.7978845608028654
gelu_cubic = 0.044715
LANES = 256
SMALL_ROWS = 16
ID_ROWS = 16


def gelu_pair(pre_act):
    inner_arg = gelu_scale * (pre_act + gelu_cubic * pre_act * pre_act * pre_act)
    tangent = jnp.tanh(inner_arg)
    activation = 0.5 * pre_act * (1.0 + tangent)
    derivative = 0.5 * (1.0 + tangent) + 0.5 * pre_act * (1.0 - tangent * tangent) * gelu_scale * (
        1.0 + 3.0 * gelu_cubic * pre_act * pre_act
    )
    return (activation, derivative)


def tap_sum(padded, kernel, tap_spacing, row_count, flipped):
    tap_count = kernel.shape[0]
    running = jnp.zeros((row_count, padded.shape[1]), jnp.float32)
    for tap_index in range(tap_count):
        source = tap_count - 1 - tap_index if flipped else tap_index
        window = padded[source * tap_spacing : source * tap_spacing + row_count].astype(jnp.float32)
        running = running + kernel[tap_index].astype(jnp.float32) * window
    return running


def tap_products(grad_pre, padded, tap_spacing, tap_count):
    row_count = grad_pre.shape[0]
    grad_wide = grad_pre.astype(jnp.float32)
    output_rows = []
    for tap_index in range(tap_count):
        window = padded[tap_index * tap_spacing : tap_index * tap_spacing + row_count].astype(
            jnp.float32
        )
        output_rows.append(jnp.sum(grad_wide * window, axis=0))
    return jnp.stack(output_rows)


def covered_at(positions, span_start, span_length):
    span_end = span_start + span_length
    within = (positions[:, None] >= span_start[None, :]) & (positions[:, None] < span_end[None, :])
    return jnp.any(within, axis=1)


def seq_shift(cells, step):
    count = lax.axis_size(SEQ)
    if step > 0:
        return lax.ppermute(cells, SEQ, [(i, i + 1) for i in range(count - 1)])
    return lax.ppermute(cells, SEQ, [(i + 1, i) for i in range(count - 1)])


def ring_copies(slab):
    count = lax.axis_size("zh")
    moved = [slab]
    for step in (1, 3, 2):
        moved.append(lax.ppermute(slab, "zh", [(i, (i + step) % count) for i in range(count)]))
    return moved


def core_swap(cells):
    return lax.ppermute(cells, "core", [(0, 1), (1, 0)])


def block_order():
    ring = lax.axis_size("zh")
    here, core = lax.axis_index("zh"), lax.axis_index("core")
    steps = jnp.array([0, 1, 3, 2], jnp.int32)
    chips = (here - steps) % ring
    return jnp.concatenate([chips * 2 + core, chips * 2 + 1 - core])


def ordered_weights(weight_rows, order):
    blocks = weight_rows.reshape(LANES, -1, LANES).transpose(1, 2, 0)
    return jnp.take(blocks, order, axis=0)


def product_over_blocks(mine, other, weights):
    half = mine.shape[0]
    total = None
    for index in range(2 * half):
        piece = mine[index] if index < half else other[index - half]
        term = jnp.dot(piece, weights[index], preferred_element_type=jnp.float32)
        total = term if total is None else total + term
    return total


def upper_kernel(mine, other, weights, slope, base, taps, grad_out, up_out, wide):
    rows = base.shape[0]
    reach = (slope.shape[0] - rows) // 2
    grad = product_over_blocks(mine, other, weights) * slope[...]
    grad = grad.astype(jnp.bfloat16)
    grad_out[...] = grad[:rows]
    grad = grad.astype(jnp.float32)
    wide[reach : reach + rows] = grad[:rows]
    wide[:reach] = grad[rows : rows + reach]
    wide[reach + rows :] = grad[rows + reach :]
    running = base[...]
    count = taps.shape[0]
    spacing = reach // (count // 2)
    for index in range(count):
        start = (count - 1 - index) * spacing
        running = running + taps[index : index + 1] * wide[start : start + rows]
    up_out[...] = running.astype(jnp.bfloat16)


def lower_kernel(mine, other, weights, slope, hot, up_row, table, taps, grad_out, small_out):
    grad = (product_over_blocks(mine, other, weights) * slope[...]).astype(jnp.bfloat16)
    grad_out[...] = grad
    count = taps.shape[0]
    picked = jnp.dot(hot[...], grad, preferred_element_type=jnp.float32)
    middle = count // 2
    embed = jnp.dot(
        hot[middle * 8 : middle * 8 + 8], up_row[...], preferred_element_type=jnp.float32
    )
    small_out[...] = jnp.zeros_like(small_out)
    for index in range(count):
        piece = picked[index * 8 : index * 8 + 8]
        small_out[index : index + 1] = jnp.sum(piece * table[...], axis=0, keepdims=True)
        embed = embed + piece * taps[index : index + 1]
    small_out[count : count + 5] = embed[:5]


def outer_kernel(act, mine, other, small, out):
    rows = act.shape[1]
    half = mine.shape[0]
    for index in range(2 * half):
        piece = mine[index, :rows] if index < half else other[index - half, :rows]
        out[:, index * LANES : (index + 1) * LANES] = jnp.dot(
            act[...], piece, preferred_element_type=jnp.float32
        ).astype(jnp.bfloat16)
    extra = small[...].astype(jnp.bfloat16)
    extra = jnp.concatenate([extra, jnp.zeros_like(extra)], axis=0)
    group = 2 * small.shape[0]
    for index in range(act.shape[0] // group):
        out[index * group : (index + 1) * group, 2 * half * LANES :] = extra


def call(kernel, outs, scratch, *operands):
    return pl.pallas_call(
        kernel,
        out_shape=outs,
        scratch_shapes=scratch,
        compiler_params=pltpu.CompilerParams(vmem_limit_bytes=32 << 20),
    )(*operands)


def scatter_first(outer):
    near = lax.axis_size(NEAR)
    pieces = outer.reshape(near, outer.shape[0] // near, outer.shape[1])
    return lax.all_to_all(pieces, NEAR, 0, 0)


def scatter_second(pieces, scale):
    far = lax.axis_size(FAR)
    total = jnp.sum(pieces.astype(jnp.float32), axis=0)
    rows = total.shape[0]
    own = rows // far
    width = total.shape[1] - LANES
    main = total[:, :width].astype(jnp.bfloat16).reshape(far, own, width)
    small = total[:SMALL_ROWS, width:].astype(jnp.bfloat16).reshape(1, own, -1)
    small = jnp.broadcast_to(small, (far,) + small.shape[1:])
    pieces = lax.all_to_all(jnp.concatenate([main, small], axis=2), FAR, 0, 0)
    total = jnp.sum(pieces.astype(jnp.float32), axis=0) * scale
    return total[:, :width], total[:, width:].reshape(SMALL_ROWS, LANES)


def on_device(
    base_ids, span_start, span_length, embedding, conv_kernel, mix_weight, saved_input, cotangent
):
    rows = saved_input.shape[0]
    tap_count = conv_kernel.shape[1]
    side = tap_count // 2
    vocab_rows = embedding.shape[0]
    total_rows = rows * lax.axis_size(SEQ)
    grad_scale = 1.0 / math.sqrt(total_rows)
    low_gap, high_gap = BASE_DILATION, 2 * BASE_DILATION
    low_reach, high_reach = side * low_gap, side * high_gap
    bf16, f32 = jnp.bfloat16, jnp.float32

    gathered = ring_copies(cotangent)

    def edge(lo, hi, cut):
        ids = jnp.broadcast_to(base_ids[cut].astype(bf16)[:, None], (ID_ROWS, LANES))
        return jnp.concatenate([saved_input[lo], cotangent[hi], ids])

    wide_edge, thin_edge = 2 * high_reach, high_reach
    to_next = edge(
        slice(rows - wide_edge, rows), slice(rows - thin_edge, rows), slice(rows - ID_ROWS, rows)
    )
    to_prev = edge(slice(0, wide_edge), slice(0, thin_edge), slice(0, ID_ROWS))
    before = seq_shift(to_next, 1)
    after = seq_shift(to_prev, -1)

    edges = jnp.concatenate(
        [before[wide_edge : wide_edge + thin_edge], after[wide_edge : wide_edge + thin_edge]]
    )
    edges_gathered = ring_copies(edges)
    mine = jnp.stack(
        [jnp.concatenate([a, b], axis=0) for a, b in zip(gathered, edges_gathered)]
    )
    other = core_swap(mine)

    first_row = lax.axis_index(SEQ) * rows
    positions = first_row - high_reach + jnp.arange(rows + 2 * high_reach, dtype=jnp.int32)
    covered = covered_at(positions, span_start, span_length)
    inner = covered[high_reach : high_reach + rows]

    def edge_last(cells):
        return jnp.concatenate(
            [cells[high_reach : high_reach + rows], cells[:high_reach], cells[high_reach + rows :]]
        )

    order = block_order()
    upper_weights = ordered_weights(mix_weight[1], order)
    lower_weights = ordered_weights(mix_weight[0], order)
    kernel_wide = conv_kernel.astype(f32)

    channel = jnp.arange(LANES, dtype=jnp.int32)
    near, far = lax.axis_size(NEAR), lax.axis_size(FAR)
    own = LANES // (near * far)
    place = (channel // own % near) * (far * own) + channel // (own * near) * own + channel % own
    shuffle = (place[None, :] == channel[:, None]).astype(bf16)

    saved_wide = jnp.concatenate([before[:wide_edge], saved_input, after[:wide_edge]])
    pre_upper = tap_sum(saved_wide, conv_kernel[1], high_gap, rows + 2 * high_reach, False)
    act_upper, slope_upper = gelu_pair(pre_upper)
    slope_upper = edge_last(jnp.where(covered[:, None], slope_upper, 0.0))
    act_upper = jnp.where(
        inner[:, None], act_upper[high_reach : high_reach + rows].astype(bf16), jnp.zeros((), bf16)
    )
    act_upper = jnp.einsum("pc,tc->pt", shuffle, act_upper, preferred_element_type=f32).astype(bf16)
    masked = jnp.where(inner[:, None], cotangent, jnp.zeros_like(cotangent)).astype(f32)

    near_positions = positions[high_reach - low_reach : high_reach + rows + low_reach]
    near_covered = covered[high_reach - low_reach : high_reach + rows + low_reach]
    ids = jnp.concatenate(
        [
            before[wide_edge + thin_edge :, 0].astype(jnp.int32),
            base_ids,
            after[wide_edge + thin_edge :, 0].astype(jnp.int32),
        ]
    )
    ids = jnp.where(near_covered, mask_token, ids)
    ids = jnp.where((near_positions >= 0) & (near_positions < total_rows), ids, 7)
    hot = (jnp.arange(8, dtype=jnp.int32)[:, None] == ids[None, :]).astype(bf16)
    hot = jnp.where(jnp.arange(8)[:, None] < vocab_rows, hot, jnp.zeros((), bf16))
    table = jnp.concatenate([embedding, jnp.zeros((8 - vocab_rows, LANES), bf16)])
    first_wide = jnp.einsum("vt,vc->tc", hot, table, preferred_element_type=f32).astype(bf16)
    pre_lower = tap_sum(first_wide, conv_kernel[0], low_gap, rows, False)
    act_lower, slope_lower = gelu_pair(pre_lower)
    act_lower = jnp.einsum(
        "pc,tc->pt", shuffle, act_lower.astype(bf16), preferred_element_type=f32
    ).astype(bf16)
    hot_taps = jnp.concatenate(
        [hot[:, index * low_gap : index * low_gap + rows] for index in range(tap_count)]
    )

    (
        slope_upper,
        act_upper,
        slope_lower,
        act_lower,
        upper_weights,
        lower_weights,
        masked,
        hot_taps,
        mine,
    ) = lax.optimization_barrier(
        (
            slope_upper,
            act_upper,
            slope_lower,
            act_lower,
            upper_weights,
            lower_weights,
            masked,
            hot_taps,
            mine,
        )
    )

    slab = jax.ShapeDtypeStruct((rows, LANES), bf16)
    small_shape = jax.ShapeDtypeStruct((SMALL_ROWS, LANES), f32)
    outer_shape = jax.ShapeDtypeStruct((LANES, 9 * LANES), bf16)
    grad_upper, up_mid = call(
        upper_kernel,
        (slab, slab),
        [pltpu.VMEM((rows + 2 * high_reach, LANES), f32)],
        mine, other, upper_weights, slope_upper, masked, kernel_wide[1],
    )

    mid_gathered = jnp.stack(ring_copies(up_mid))
    mid_other = core_swap(mid_gathered)

    upper_taps = tap_products(
        grad_upper, saved_wide[high_reach : rows + 3 * high_reach], high_gap, tap_count
    )
    upper_small = jnp.concatenate([upper_taps, jnp.zeros((SMALL_ROWS - tap_count, LANES), f32)])
    upper_outer = call(outer_kernel, outer_shape, [], act_upper, mine, other, upper_small)
    upper_grad, upper_small = scatter_second(scatter_first(upper_outer), grad_scale)

    grad_lower, lower_small = call(
        lower_kernel,
        (slab, small_shape),
        [],
        mid_gathered, mid_other, lower_weights, slope_lower, hot_taps, up_mid,
        table.astype(f32), kernel_wide[0],
    )
    lower_outer = call(
        outer_kernel, outer_shape, [], act_lower, mid_gathered, mid_other, lower_small
    )
    lower_grad, lower_small = scatter_second(scatter_first(lower_outer), grad_scale)

    padded = jnp.concatenate(
        [
            seq_shift(grad_lower[rows - low_reach :], 1),
            grad_lower,
            seq_shift(grad_lower[:low_reach], -1),
        ]
    )
    input_grad = (
        up_mid.astype(f32) + tap_sum(padded, conv_kernel[0], low_gap, rows, True)
    ).astype(bf16)

    blocks = jnp.stack([lower_grad, upper_grad]).reshape(2, own, -1, LANES)
    spots = jnp.argsort(order)
    weight_grad = jnp.take(blocks, spots, axis=2).reshape(2, own, -1)
    kernel_grad = jnp.stack([lower_small[:tap_count], upper_small[:tap_count]])
    embed_grad = lower_small[tap_count : tap_count + vocab_rows]
    return (input_grad, weight_grad, kernel_grad, embed_grad)


def solution(mesh):
    fine = Mesh(mesh.devices.reshape(8, 2, 4, 4, 2), SEQ + BLK)
    placed = (
        P(SEQ),
        P(),
        P(),
        P(None, BLK),
        P(None, None, BLK),
        P(None, BLK, None),
        P(SEQ, BLK),
        P(SEQ, BLK),
    )
    return jax.shard_map(
        on_device,
        mesh=fine,
        in_specs=placed,
        out_specs=(
            P(SEQ, BLK),
            P(None, BLK + SEQ, None),
            P(None, None, BLK),
            P(None, BLK),
        ),
        check_vma=False,
    )
```

```python
import math

import jax
import jax.numpy as jnp
from jax import lax
from jax.experimental import pallas as pl
from jax.experimental.pallas import tpu as pltpu
from jax.sharding import Mesh, PartitionSpec as P

BASE_DILATION = 4

SEQ = ("y", "zl", "x")
BLK = ("zh", "core")
NEAR = ("zl", "x")
STEPS = (0, 1, 3, 2)

mask_token = 4
gelu_scale = 0.7978845608028654
gelu_cubic = 0.044715
LANES = 256
BF16 = jnp.bfloat16
F32 = jnp.float32

ROWS = 512
TAPS = 9
VOCAB = 5
LOW_GAP, HIGH_GAP = BASE_DILATION, 2 * BASE_DILATION
LOW_REACH, HIGH_REACH = 4 * LOW_GAP, 4 * HIGH_GAP
EDGE = HIGH_REACH
MESSAGE = EDGE + 16
CHUNK = 64
PAIRED = (((1,), (1,)), ((), ()))


def gelu_pair(pre_act):
    square = pre_act * pre_act
    tangent = jnp.tanh(gelu_scale * (pre_act + gelu_cubic * square * pre_act))
    half = 0.5 * (1.0 + tangent)
    derivative = half + 0.5 * pre_act * (1.0 - tangent * tangent) * gelu_scale * (
        1.0 + 3.0 * gelu_cubic * square
    )
    return (pre_act * half, derivative)


def call(kernel, outs, scratch, in_specs, *operands):
    extra = {} if in_specs is None else {"in_specs": in_specs, "grid": (1,)}
    return pl.pallas_call(
        kernel,
        out_shape=outs,
        scratch_shapes=scratch,
        compiler_params=pltpu.CompilerParams(vmem_limit_bytes=40 << 20),
        **extra,
    )(*operands)


def shape(dims, kind):
    return jax.ShapeDtypeStruct(dims, kind)


def pack_kernel(saved_head, saved_tail, ids, next_out, prev_out):
    for out, rows, row in ((next_out, saved_tail, 3), (prev_out, saved_head, 0)):
        out[:EDGE] = rows[...]
        line = jnp.broadcast_to(ids[row : row + 1].astype(F32), (MESSAGE - EDGE, 128))
        out[EDGE:] = jnp.concatenate([line, line], axis=1).astype(BF16)


def prep_kernel(
    place, before, after, saved, cot, ids, start, length, embedding, conv,
    slope_up, act_up, slope_low, act_low, masked, hot_out,
    cover, idw, wide, first, table, act_all,
):
    base = place[0] * ROWS - CHUNK
    total = place[1]

    def cover_chunk(index, carry):
        row0 = pl.multiple_of(index * CHUNK, CHUNK)
        here = lax.broadcasted_iota(jnp.int32, (CHUNK, 128), 0) + (base + row0)
        hit = jnp.zeros((CHUNK, 128), jnp.int32)
        for group in range(start.shape[0]):
            gap = here - start[group : group + 1]
            hit = jnp.where((gap >= 0) & (gap < length[group : group + 1]), 1, hit)
        seen = jnp.max(hit, axis=1, keepdims=True).astype(F32)
        cover[pl.ds(row0, CHUNK), :] = jnp.broadcast_to(seen, (CHUNK, 128))
        return carry

    lax.fori_loop(0, ROWS // CHUNK + 2, cover_chunk, 0)

    def column(row):
        return jnp.transpose(jnp.broadcast_to(row.astype(F32), (128, 128)))

    idw[:LOW_REACH] = column(before[EDGE : EDGE + 1, :128])[128 - LOW_REACH :]
    for piece in range(ROWS // 128):
        idw[LOW_REACH + 128 * piece : LOW_REACH + 128 * (piece + 1)] = column(ids[piece : piece + 1])
    idw[LOW_REACH + ROWS :] = column(after[EDGE : EDGE + 1, :128])[:LOW_REACH]
    spread = ROWS + 2 * LOW_REACH
    spot = lax.broadcasted_iota(jnp.int32, (spread, 128), 0) + (base + CHUNK - LOW_REACH)
    lane = lax.broadcasted_iota(jnp.int32, (1, 128), 1)
    tokens = jnp.where(
        cover[CHUNK - LOW_REACH : CHUNK - LOW_REACH + spread] > 0.0,
        float(mask_token),
        idw[...],
    )
    tokens = jnp.where((spot >= 0) & (spot < total), tokens, 7.0)
    idw[...] = tokens
    table[...] = jnp.zeros_like(table)
    table[:VOCAB] = embedding[...].astype(F32)
    hot = jnp.where(tokens == lane.astype(F32), 1.0, 0.0).astype(BF16)
    first[...] = jnp.dot(hot, table[...].astype(BF16), preferred_element_type=F32)

    channel = lax.broadcasted_iota(jnp.int32, (LANES, LANES), 1)
    target = lax.broadcasted_iota(jnp.int32, (LANES, LANES), 0)
    tail = ((channel >> 5) << 2) | (channel & 3)
    low_place = (((channel >> 2) & 7) << 5) | tail
    up_place = (((channel >> 2) & 3) << 6) | (((channel >> 4) & 1) << 5) | tail
    low_shuffle = jnp.where(low_place == target, 1.0, 0.0).astype(BF16)
    up_shuffle = jnp.where(up_place == target, 1.0, 0.0).astype(BF16)

    taps_low = [conv[0, index : index + 1].astype(F32) for index in range(TAPS)]
    for chunk in range(ROWS // CHUNK):
        row0 = chunk * CHUNK
        pre = None
        for index in range(TAPS):
            begin = row0 + index * LOW_GAP
            term = taps_low[index] * first[begin : begin + CHUNK]
            pre = term if pre is None else pre + term
        act, slope = gelu_pair(pre)
        slope_low[row0 : row0 + CHUNK] = slope
        act_all[row0 : row0 + CHUNK] = act.astype(BF16)
    act_low[...] = lax.dot_general(
        low_shuffle, act_all[:ROWS], PAIRED, preferred_element_type=F32
    ).astype(BF16)

    picked = idw[:ROWS]
    for index in range(1, TAPS):
        picked = jnp.where((lane >> 3) == index, idw[index * LOW_GAP : index * LOW_GAP + ROWS], picked)
    kind = lane & 7
    live = (kind < VOCAB) & (lane < 8 * TAPS)
    hot = jnp.where((picked == kind.astype(F32)) & live, 1.0, 0.0)
    hot_out[...] = jnp.transpose(hot).astype(BF16)

    wide[:HIGH_REACH] = before[:HIGH_REACH].astype(F32)
    wide[HIGH_REACH : HIGH_REACH + ROWS] = saved[...].astype(F32)
    wide[HIGH_REACH + ROWS :] = after[:HIGH_REACH].astype(F32)
    taps_up = [conv[1, index : index + 1].astype(F32) for index in range(TAPS)]
    for chunk in range(ROWS // CHUNK):
        row0 = chunk * CHUNK
        pre = None
        for index in range(TAPS):
            begin = row0 + index * HIGH_GAP
            term = taps_up[index] * wide[begin : begin + CHUNK]
            pre = term if pre is None else pre + term
        act, slope = gelu_pair(pre)
        seen = cover[CHUNK + row0 : 2 * CHUNK + row0] > 0.0
        seen = jnp.concatenate([seen, seen], axis=1)
        slope_up[row0 : row0 + CHUNK] = jnp.where(seen, slope, 0.0)
        act_all[row0 : row0 + CHUNK] = jnp.where(seen, act, 0.0).astype(BF16)
        masked[row0 : row0 + CHUNK] = jnp.where(
            seen, cot[row0 : row0 + CHUNK].astype(F32), 0.0
        ).astype(BF16)
    act_up[...] = lax.dot_general(
        up_shuffle, act_all[:ROWS], PAIRED, preferred_element_type=F32
    ).astype(BF16)


def chip_block(place, step):
    return (place[2] - step) & 3


def weight_columns(weights, place, step, core):
    block = chip_block(place, step) * 2 + core
    return weights[0, :, pl.ds(pl.multiple_of(block * LANES, LANES), LANES)]


def product_over_blocks(place, mine, pairs, weights):
    total = None
    for index, step in enumerate(STEPS):
        term = lax.dot_general(
            mine[index][...], weight_columns(weights, place, step, place[3]), PAIRED,
            preferred_element_type=F32,
        )
        total = term if total is None else total + term
    for index, step in enumerate(STEPS):
        total = total + lax.dot_general(
            pairs[index // 2][index % 2], weight_columns(weights, place, step, 1 - place[3]),
            PAIRED, preferred_element_type=F32,
        )
    return total


def upper_kernel(place, m0, m1, m2, m3, p0, p1, weights, slope, grad_out, head_out, tail_out):
    grad = product_over_blocks(place, (m0, m1, m2, m3), (p0, p1), weights) * slope[...]
    grad = grad.astype(BF16)
    grad_out[...] = grad
    head_out[...] = grad[:HIGH_REACH]
    tail_out[...] = grad[ROWS - HIGH_REACH :]


def outer_product(act, mine, pairs, out):
    for index in range(2 * len(STEPS)):
        half = index % len(STEPS)
        piece = mine[half][...] if index < len(STEPS) else pairs[half // 2][half % 2]
        out[:, index * LANES : (index + 1) * LANES] = jnp.dot(
            act[...], piece, preferred_element_type=F32
        ).astype(BF16)


def upper_outer_kernel(act, m0, m1, m2, m3, p0, p1, grad, before, saved, after, out, tap_out, wide):
    outer_product(act, (m0, m1, m2, m3), (p0, p1), out)
    wide[:HIGH_REACH] = before[:HIGH_REACH].astype(F32)
    wide[HIGH_REACH : HIGH_REACH + ROWS] = saved[...].astype(F32)
    wide[HIGH_REACH + ROWS :] = after[:HIGH_REACH].astype(F32)
    sums = [jnp.zeros((8, LANES), F32) for index in range(TAPS)]
    for chunk in range(ROWS // CHUNK):
        row0 = chunk * CHUNK
        grad_wide = grad[row0 : row0 + CHUNK].astype(F32)
        for index in range(TAPS):
            begin = row0 + index * HIGH_GAP
            term = grad_wide * wide[begin : begin + CHUNK]
            sums[index] = sums[index] + jnp.sum(term.reshape(CHUNK // 8, 8, LANES), axis=0)
    tap_out[...] = jnp.zeros_like(tap_out)
    for index in range(TAPS):
        tap_out[index : index + 1] = jnp.sum(sums[index], axis=0, keepdims=True)


def lower_kernel(
    place, act, m0, m1, m2, m3, p0, p1, weights, slope, hot, up_row, embedding, conv, upper_taps,
    out, grad_out, small, table,
):
    mine, pairs = (m0, m1, m2, m3), (p0, p1)
    grad = (product_over_blocks(place, mine, pairs, weights) * slope[...]).astype(BF16)
    grad_out[...] = grad
    outer_product(act, mine, pairs, out)
    picked = jnp.dot(hot[...], grad, preferred_element_type=F32)
    embed = jnp.dot(hot[32:48], up_row[...], preferred_element_type=F32)[:8]
    table[...] = jnp.zeros_like(table)
    table[:VOCAB] = embedding[...].astype(F32)
    small[...] = jnp.zeros_like(small)
    for index in range(TAPS):
        piece = picked[index * 8 : index * 8 + 8]
        small[index : index + 1] = jnp.sum(piece * table[...], axis=0, keepdims=True)
        embed = embed + piece * conv[0, index : index + 1].astype(F32)
    small[TAPS : TAPS + VOCAB] = embed[:VOCAB]
    small[TAPS + VOCAB : 2 * TAPS + VOCAB] = upper_taps[:TAPS]
    packed = small[...].astype(BF16)
    for index in range(LANES // 32):
        out[index * 32 : (index + 1) * 32, 8 * LANES :] = packed


def upper_half_kernel(place, pieces, keep, send, total):
    running = pieces[0].astype(F32)
    for index in range(1, pieces.shape[0]):
        running = running + pieces[index].astype(F32)
    total[...] = running
    keep[...] = total[pl.ds(pl.multiple_of(place[4] * 32, 32), 32), :]
    send[...] = total[pl.ds(pl.multiple_of((1 - place[4]) * 32, 32), 32), :].astype(BF16)


def middle_kernel(pieces, keep, received, out):
    running = pieces[0].astype(F32)
    for index in range(1, pieces.shape[0]):
        running = running + pieces[index].astype(F32)
    width = 8 * LANES
    upper = (keep[...] + received[...].astype(F32)).astype(BF16)
    small = running[:, width:].astype(BF16)
    lower = running[:, :width].astype(BF16)
    for far in range(8):
        out[far, :, :width] = lower[4 * far : 4 * far + 4]
        out[far, :, width : 2 * width] = upper[4 * far : 4 * far + 4]
        for group in range(6):
            begin = 2 * width + group * LANES
            out[far, :, begin : begin + LANES] = small[4 * group : 4 * group + 4]


def final_kernel(place, pieces, weight_out, kernel_out, embed_out, *, scale):
    running = pieces[0].astype(F32)
    for index in range(1, pieces.shape[0]):
        running = running + pieces[index].astype(F32)
    running = running * scale
    width = 8 * LANES
    for index in range(8):
        step = STEPS[index % 4]
        core = place[3] if index < 4 else 1 - place[3]
        spot = pl.multiple_of((chip_block(place, step) * 2 + core) * LANES, LANES)
        for layer in range(2):
            begin = layer * width + index * LANES
            weight_out[layer, :, pl.ds(spot, LANES)] = running[:, begin : begin + LANES]

    def small_row(row):
        begin = 2 * width + (row // 4) * LANES
        return running[row % 4 : row % 4 + 1, begin : begin + LANES]

    for index in range(TAPS):
        kernel_out[0, index : index + 1] = small_row(index)
        kernel_out[1, index : index + 1] = small_row(TAPS + VOCAB + index)
    for index in range(VOCAB):
        embed_out[index : index + 1] = small_row(TAPS + index)


def spread_kernel(base, grad, before, after, conv, out, wide, *, layer, gap):
    reach = gap * (TAPS // 2)
    wide[:reach] = before[...].astype(F32)
    wide[reach : reach + ROWS] = grad[...].astype(F32)
    wide[reach + ROWS :] = after[...].astype(F32)
    for chunk in range(ROWS // CHUNK):
        row0 = chunk * CHUNK
        running = base[row0 : row0 + CHUNK].astype(F32)
        for index in range(TAPS):
            begin = row0 + (TAPS - 1 - index) * gap
            tap = conv[layer, index : index + 1].astype(F32)
            running = running + tap * wide[begin : begin + CHUNK]
        out[row0 : row0 + CHUNK] = running.astype(BF16)


def spread(base, grad, before, after, conv, layer, gap):
    def kernel(*refs):
        spread_kernel(*refs, layer=layer, gap=gap)

    scratch = [pltpu.VMEM((ROWS + gap * (TAPS - 1), LANES), F32)]
    out = shape((ROWS, LANES), BF16)
    return call(kernel, out, scratch, None, base, grad, before, after, conv)


def seq_shift(cells, step):
    count = lax.axis_size(SEQ)
    if step > 0:
        return lax.ppermute(cells, SEQ, [(i, i + 1) for i in range(count - 1)])
    return lax.ppermute(cells, SEQ, [(i + 1, i) for i in range(count - 1)])


def ring_copies(slab):
    count = lax.axis_size("zh")
    moved = {0: slab}
    for step in (2, 1, 3):
        moved[step] = lax.ppermute(slab, "zh", [(i, (i + step) % count) for i in range(count)])
    return [moved[step] for step in STEPS]


def core_swap(cells):
    return lax.ppermute(cells, "core", [(0, 1), (1, 0)])


def swapped_pairs(mine):
    return core_swap(jnp.stack(mine[:2])), core_swap(jnp.stack(mine[2:]))


def on_device(
    base_ids, span_start, span_length, embedding, conv_kernel, mix_weight, saved_input, cotangent
):
    total_rows = ROWS * lax.axis_size(SEQ)
    place = jnp.stack(
        [
            lax.axis_index(SEQ),
            jnp.int32(total_rows),
            lax.axis_index("zh"),
            lax.axis_index("core"),
            lax.axis_index("zl"),
        ]
    ).astype(jnp.int32)
    smem = pl.BlockSpec(memory_space=pltpu.SMEM)
    vmem = pl.BlockSpec(memory_space=pltpu.VMEM)
    ids = base_ids.reshape(ROWS // 128, 128)
    slab = shape((ROWS, LANES), BF16)
    slab_wide = shape((ROWS, LANES), F32)
    turned = shape((LANES, ROWS), BF16)

    message = shape((MESSAGE, LANES), BF16)
    last = ROWS // HIGH_REACH - 1
    to_next, to_prev = call(
        pack_kernel,
        (message, message),
        [],
        [
            pl.BlockSpec((HIGH_REACH, LANES), lambda step: (0, 0)),
            pl.BlockSpec((HIGH_REACH, LANES), lambda step: (last, 0)),
            vmem,
        ],
        saved_input, saved_input, ids,
    )
    before = seq_shift(to_next, 1)
    after = seq_shift(to_prev, -1)
    source, before, after = lax.optimization_barrier((cotangent, before, after))
    mine = ring_copies(source)

    slope_up, act_up, slope_low, act_low, masked, hot = call(
        prep_kernel,
        (slab_wide, turned, slab_wide, turned, slab, shape((128, ROWS), BF16)),
        [
            pltpu.VMEM((ROWS + 2 * CHUNK, 128), F32),
            pltpu.VMEM((ROWS + 2 * LOW_REACH, 128), F32),
            pltpu.VMEM((ROWS + 2 * HIGH_REACH, LANES), F32),
            pltpu.VMEM((ROWS + 2 * LOW_REACH, LANES), F32),
            pltpu.VMEM((128, LANES), F32),
            pltpu.VMEM((ROWS, LANES), BF16),
        ],
        [smem] + [vmem] * 9,
        place, before, after, saved_input, cotangent, ids,
        span_start.reshape(-1, 128), span_length.reshape(-1, 128), embedding, conv_kernel,
    )
    slope_up, mine[1], mine[2], mine[3] = lax.optimization_barrier(
        (slope_up, mine[1], mine[2], mine[3])
    )
    pairs = swapped_pairs(mine)

    weight_specs = [
        pl.BlockSpec((1, LANES, 8 * LANES), lambda step: (0, 0, 0)),
        pl.BlockSpec((1, LANES, 8 * LANES), lambda step: (1, 0, 0)),
    ]
    rim = shape((HIGH_REACH, LANES), BF16)
    grad_upper, head, tail = call(
        upper_kernel,
        (slab, rim, rim),
        [],
        [smem] + [vmem] * 6 + [weight_specs[1], vmem],
        place, *mine, *pairs, mix_weight, slope_up,
    )
    up_before = seq_shift(tail, 1)
    up_after = seq_shift(head, -1)
    up_mid = spread(masked, grad_upper, up_before, up_after, conv_kernel, 1, HIGH_GAP)
    mid = ring_copies(up_mid)
    mid_pairs = swapped_pairs(mid)

    upper_outer, upper_taps = call(
        upper_outer_kernel,
        (shape((LANES, 8 * LANES), BF16), shape((16, LANES), F32)),
        [pltpu.VMEM((ROWS + 2 * HIGH_REACH, LANES), F32)],
        None,
        act_up, *mine, *pairs, grad_upper, before, saved_input, after,
    )
    pieces = lax.all_to_all(upper_outer.reshape(4, 64, 8 * LANES), "x", 0, 0)
    keep, send = call(
        upper_half_kernel,
        (shape((32, 8 * LANES), F32), shape((32, 8 * LANES), BF16)),
        [pltpu.VMEM((64, 8 * LANES), F32)],
        [smem, vmem],
        place, pieces,
    )
    received = lax.ppermute(send, "zl", [(0, 1), (1, 0)])

    lower_outer, grad_lower = call(
        lower_kernel,
        (shape((LANES, 9 * LANES), BF16), slab),
        [pltpu.VMEM((32, LANES), F32), pltpu.VMEM((8, LANES), F32)],
        [smem] + [vmem] * 7 + [weight_specs[0]] + [vmem] * 6,
        place, act_low, *mid, *mid_pairs, mix_weight, slope_low, hot, up_mid, embedding,
        conv_kernel, upper_taps,
    )
    pieces = lax.all_to_all(lower_outer.reshape(8, 32, 9 * LANES), NEAR, 0, 0)
    low_before = seq_shift(grad_lower[ROWS - LOW_REACH :], 1)
    low_after = seq_shift(grad_lower[:LOW_REACH], -1)
    input_grad = spread(up_mid, grad_lower, low_before, low_after, conv_kernel, 0, LOW_GAP)
    middle = call(
        middle_kernel, shape((8, 4, 22 * LANES), BF16), [], None, pieces, keep, received
    )
    pieces = lax.all_to_all(middle, "y", 0, 0)

    def finish(*refs):
        final_kernel(*refs, scale=1.0 / math.sqrt(total_rows))

    weight_grad, kernel_grad, embed_grad = call(
        finish,
        (shape((2, 4, 8 * LANES), F32), shape((2, TAPS, LANES), F32), shape((VOCAB, LANES), F32)),
        [],
        [smem, vmem],
        place, pieces,
    )
    return (input_grad, weight_grad, kernel_grad, embed_grad)


def solution(mesh):
    fine = Mesh(mesh.devices.reshape(8, 2, 4, 4, 2), SEQ + BLK)
    placed = (
        P(SEQ),
        P(),
        P(),
        P(None, BLK),
        P(None, None, BLK),
        P(None, BLK, None),
        P(SEQ, BLK),
        P(SEQ, BLK),
    )
    return jax.shard_map(
        on_device,
        mesh=fine,
        in_specs=placed,
        out_specs=(
            P(SEQ, BLK),
            P(None, BLK + SEQ, None),
            P(None, None, BLK),
            P(None, BLK),
        ),
        check_vma=False,
    )
```

```python
import math

import jax
import jax.numpy as jnp
from jax import lax
from jax.experimental import pallas as pl
from jax.experimental.pallas import tpu as pltpu
from jax.sharding import Mesh, PartitionSpec as P

BASE_DILATION = 4

SEQ = ("y", "zl", "x")
BLK = ("zh", "core")
NEAR = ("zl", "x")
STEPS = (0, 1, 3, 2)

mask_token = 4
gelu_scale = 0.7978845608028654
gelu_cubic = 0.044715
LANES = 256
BF16 = jnp.bfloat16
F32 = jnp.float32

ROWS = 512
TAPS = 9
VOCAB = 5
LOW_GAP, HIGH_GAP = BASE_DILATION, 2 * BASE_DILATION
LOW_REACH, HIGH_REACH = 4 * LOW_GAP, 4 * HIGH_GAP
EDGE = HIGH_REACH
MESSAGE = EDGE + 16
CHUNK = 64
PAIRED = (((1,), (1,)), ((), ()))


def gelu_pair(pre_act):
    square = pre_act * pre_act
    tangent = jnp.tanh(gelu_scale * (pre_act + gelu_cubic * square * pre_act))
    half = 0.5 * (1.0 + tangent)
    derivative = half + 0.5 * pre_act * (1.0 - tangent * tangent) * gelu_scale * (
        1.0 + 3.0 * gelu_cubic * square
    )
    return (pre_act * half, derivative)


def call(kernel, outs, scratch, in_specs, *operands, out_specs=None):
    extra = {} if in_specs is None else {"in_specs": in_specs, "grid": (1,)}
    if out_specs is not None:
        extra["out_specs"] = out_specs
    return pl.pallas_call(
        kernel,
        out_shape=outs,
        scratch_shapes=scratch,
        compiler_params=pltpu.CompilerParams(vmem_limit_bytes=16 << 20),
        **extra,
    )(*operands)


def call_staged(kernel, outs, scratch, place, *operands):
    count = len(operands)
    lead = 0 if place is None else 1

    def staged(*refs):
        head, sources, rest = refs[:lead], refs[lead : lead + count], refs[lead + count :]
        held, sems = rest[-count - 1 : -1], rest[-1]
        loads = [
            pltpu.make_async_copy(sources[index], held[index], sems.at[index])
            for index in range(count)
        ]
        for load in loads:
            load.start()
        for load in loads:
            load.wait()
        kernel(*head, *held, *rest[: -count - 1])

    smem = pl.BlockSpec(memory_space=pltpu.SMEM)
    hbm = pl.BlockSpec(memory_space=pltpu.HBM)
    operands = [pltpu.with_memory_space_constraint(cells, pltpu.HBM) for cells in operands]
    return pl.pallas_call(
        staged,
        out_shape=outs,
        in_specs=[smem] * lead + [hbm] * count,
        scratch_shapes=list(scratch)
        + [pltpu.VMEM(cells.shape, cells.dtype) for cells in operands]
        + [pltpu.SemaphoreType.DMA((count,))],
        compiler_params=pltpu.CompilerParams(vmem_limit_bytes=24 << 20),
    )(*(() if place is None else (place,)), *operands)


def shape(dims, kind):
    return jax.ShapeDtypeStruct(dims, kind)


def pack_kernel(saved, ids, next_out, prev_out):
    for out, begin, row in ((next_out, ROWS - EDGE, 3), (prev_out, 0, 0)):
        out[:EDGE] = saved[begin : begin + EDGE]
        line = jnp.broadcast_to(ids[row : row + 1].astype(F32), (MESSAGE - EDGE, 128))
        out[EDGE:] = jnp.concatenate([line, line], axis=1).astype(BF16)


def prep_kernel(
    place, before, after, saved, cot, ids, start, length, embedding, conv,
    slope_up, act_up, slope_low, act_low, masked, hot_out,
    cover, idw, wide, first, table, act_all,
):
    base = place[0] * ROWS - CHUNK
    total = place[1]

    def cover_chunk(index, carry):
        row0 = pl.multiple_of(index * CHUNK, CHUNK)
        here = lax.broadcasted_iota(jnp.int32, (CHUNK, 128), 0) + (base + row0)
        hit = jnp.zeros((CHUNK, 128), jnp.int32)
        for group in range(start.shape[0]):
            gap = here - start[group : group + 1]
            hit = jnp.where((gap >= 0) & (gap < length[group : group + 1]), 1, hit)
        seen = jnp.max(hit, axis=1, keepdims=True).astype(F32)
        cover[pl.ds(row0, CHUNK), :] = jnp.broadcast_to(seen, (CHUNK, 128))
        return carry

    lax.fori_loop(0, ROWS // CHUNK + 2, cover_chunk, 0)

    def column(row):
        return jnp.transpose(jnp.broadcast_to(row.astype(F32), (128, 128)))

    idw[:LOW_REACH] = column(before[EDGE : EDGE + 1, :128])[128 - LOW_REACH :]
    for piece in range(ROWS // 128):
        idw[LOW_REACH + 128 * piece : LOW_REACH + 128 * (piece + 1)] = column(ids[piece : piece + 1])
    idw[LOW_REACH + ROWS :] = column(after[EDGE : EDGE + 1, :128])[:LOW_REACH]
    spread = ROWS + 2 * LOW_REACH
    spot = lax.broadcasted_iota(jnp.int32, (spread, 128), 0) + (base + CHUNK - LOW_REACH)
    lane = lax.broadcasted_iota(jnp.int32, (1, 128), 1)
    tokens = jnp.where(
        cover[CHUNK - LOW_REACH : CHUNK - LOW_REACH + spread] > 0.0,
        float(mask_token),
        idw[...],
    )
    tokens = jnp.where((spot >= 0) & (spot < total), tokens, 7.0)
    idw[...] = tokens
    table[...] = jnp.zeros_like(table)
    table[:VOCAB] = embedding[...].astype(F32)
    hot = jnp.where(tokens == lane.astype(F32), 1.0, 0.0).astype(BF16)
    first[...] = jnp.dot(hot, table[...].astype(BF16), preferred_element_type=F32)

    channel = lax.broadcasted_iota(jnp.int32, (LANES, LANES), 1)
    target = lax.broadcasted_iota(jnp.int32, (LANES, LANES), 0)
    tail = ((channel >> 5) << 2) | (channel & 3)
    low_place = (((channel >> 2) & 7) << 5) | tail
    up_place = (((channel >> 2) & 3) << 6) | (((channel >> 4) & 1) << 5) | tail
    low_shuffle = jnp.where(low_place == target, 1.0, 0.0).astype(BF16)
    up_shuffle = jnp.where(up_place == target, 1.0, 0.0).astype(BF16)

    taps_low = [conv[0, index : index + 1].astype(F32) for index in range(TAPS)]
    for chunk in range(ROWS // CHUNK):
        row0 = chunk * CHUNK
        pre = None
        for index in range(TAPS):
            begin = row0 + index * LOW_GAP
            term = taps_low[index] * first[begin : begin + CHUNK]
            pre = term if pre is None else pre + term
        act, slope = gelu_pair(pre)
        slope_low[row0 : row0 + CHUNK] = slope
        act_all[row0 : row0 + CHUNK] = act.astype(BF16)
    act_low[...] = lax.dot_general(
        low_shuffle, act_all[:ROWS], PAIRED, preferred_element_type=F32
    ).astype(BF16)

    picked = idw[:ROWS]
    for index in range(1, TAPS):
        picked = jnp.where((lane >> 3) == index, idw[index * LOW_GAP : index * LOW_GAP + ROWS], picked)
    kind = lane & 7
    live = (kind < VOCAB) & (lane < 8 * TAPS)
    hot = jnp.where((picked == kind.astype(F32)) & live, 1.0, 0.0)
    hot_out[...] = jnp.transpose(hot).astype(BF16)

    wide[:HIGH_REACH] = before[:HIGH_REACH].astype(F32)
    wide[HIGH_REACH : HIGH_REACH + ROWS] = saved[...].astype(F32)
    wide[HIGH_REACH + ROWS :] = after[:HIGH_REACH].astype(F32)
    taps_up = [conv[1, index : index + 1].astype(F32) for index in range(TAPS)]
    for chunk in range(ROWS // CHUNK):
        row0 = chunk * CHUNK
        pre = None
        for index in range(TAPS):
            begin = row0 + index * HIGH_GAP
            term = taps_up[index] * wide[begin : begin + CHUNK]
            pre = term if pre is None else pre + term
        act, slope = gelu_pair(pre)
        seen = cover[CHUNK + row0 : 2 * CHUNK + row0] > 0.0
        seen = jnp.concatenate([seen, seen], axis=1)
        slope_up[row0 : row0 + CHUNK] = jnp.where(seen, slope, 0.0)
        act_all[row0 : row0 + CHUNK] = jnp.where(seen, act, 0.0).astype(BF16)
        masked[row0 : row0 + CHUNK] = jnp.where(
            seen, cot[row0 : row0 + CHUNK].astype(F32), 0.0
        ).astype(BF16)
    act_up[...] = lax.dot_general(
        up_shuffle, act_all[:ROWS], PAIRED, preferred_element_type=F32
    ).astype(BF16)


def chip_block(place, step):
    return (place[2] - step) & 3


def weight_columns(weights, place, step, core):
    block = chip_block(place, step) * 2 + core
    return weights[0, :, pl.ds(pl.multiple_of(block * LANES, LANES), LANES)]


def product_over_blocks(place, mine, pairs, weights):
    total = None
    for index, step in enumerate(STEPS):
        term = lax.dot_general(
            mine[index][...], weight_columns(weights, place, step, place[3]), PAIRED,
            preferred_element_type=F32,
        )
        total = term if total is None else total + term
    for index, step in enumerate(STEPS):
        total = total + lax.dot_general(
            pairs[index // 2][index % 2], weight_columns(weights, place, step, 1 - place[3]),
            PAIRED, preferred_element_type=F32,
        )
    return total


def upper_kernel(place, m0, m1, m2, m3, p0, p1, weights, slope, grad_out, head_out, tail_out):
    grad = product_over_blocks(place, (m0, m1, m2, m3), (p0, p1), weights) * slope[...]
    grad = grad.astype(BF16)
    grad_out[...] = grad
    head_out[...] = grad[:HIGH_REACH]
    tail_out[...] = grad[ROWS - HIGH_REACH :]


def outer_product(act, mine, pairs, out, stage, sems):
    copies = []
    for index in range(2 * len(STEPS)):
        half = index % len(STEPS)
        piece = mine[half][...] if index < len(STEPS) else pairs[half // 2][half % 2]
        lanes = slice(index * LANES, (index + 1) * LANES)
        stage[:, lanes] = jnp.dot(act[...], piece, preferred_element_type=F32).astype(BF16)
        copies.append(
            pltpu.make_async_copy(stage.at[:, lanes], out.at[:, lanes], sems.at[index])
        )
        copies[-1].start()
    return copies


def upper_outer_kernel(
    act, m0, m1, m2, m3, p0, p1, grad, before, saved, after, out, tap_out, wide, stage, sems
):
    copies = outer_product(act, (m0, m1, m2, m3), (p0, p1), out, stage, sems)
    wide[:HIGH_REACH] = before[:HIGH_REACH].astype(F32)
    wide[HIGH_REACH : HIGH_REACH + ROWS] = saved[...].astype(F32)
    wide[HIGH_REACH + ROWS :] = after[:HIGH_REACH].astype(F32)
    sums = [jnp.zeros((8, LANES), F32) for index in range(TAPS)]
    for chunk in range(ROWS // CHUNK):
        row0 = chunk * CHUNK
        grad_wide = grad[row0 : row0 + CHUNK].astype(F32)
        for index in range(TAPS):
            begin = row0 + index * HIGH_GAP
            term = grad_wide * wide[begin : begin + CHUNK]
            sums[index] = sums[index] + jnp.sum(term.reshape(CHUNK // 8, 8, LANES), axis=0)
    tap_out[...] = jnp.zeros_like(tap_out)
    for index in range(TAPS):
        tap_out[index : index + 1] = jnp.sum(sums[index], axis=0, keepdims=True)
    for copy in copies:
        copy.wait()


def lower_kernel(
    place, act, m0, m1, m2, m3, p0, p1, weights, slope, hot, up_row, embedding, conv, upper_taps,
    out, grad_out, small, table, stage, sems,
):
    mine, pairs = (m0, m1, m2, m3), (p0, p1)
    grad = (product_over_blocks(place, mine, pairs, weights) * slope[...]).astype(BF16)
    grad_out[...] = grad
    copies = outer_product(act, mine, pairs, out, stage, sems)
    picked = jnp.dot(hot[...], grad, preferred_element_type=F32)
    embed = jnp.dot(hot[32:48], up_row[...], preferred_element_type=F32)[:8]
    table[...] = jnp.zeros_like(table)
    table[:VOCAB] = embedding[...].astype(F32)
    small[...] = jnp.zeros_like(small)
    for index in range(TAPS):
        piece = picked[index * 8 : index * 8 + 8]
        small[index : index + 1] = jnp.sum(piece * table[...], axis=0, keepdims=True)
        embed = embed + piece * conv[0, index : index + 1].astype(F32)
    small[TAPS : TAPS + VOCAB] = embed[:VOCAB]
    small[TAPS + VOCAB : 2 * TAPS + VOCAB] = upper_taps[:TAPS]
    packed = small[...].astype(BF16)
    for index in range(LANES // 32):
        stage[index * 32 : (index + 1) * 32, 8 * LANES :] = packed
    last = pltpu.make_async_copy(
        stage.at[:, 8 * LANES :], out.at[:, 8 * LANES :], sems.at[8]
    )
    last.start()
    for copy in copies + [last]:
        copy.wait()


def upper_half_kernel(place, pieces, keep, send, total):
    running = pieces[0].astype(F32)
    for index in range(1, pieces.shape[0]):
        running = running + pieces[index].astype(F32)
    total[...] = running
    keep[...] = total[pl.ds(pl.multiple_of(place[4] * 32, 32), 32), :]
    send[...] = total[pl.ds(pl.multiple_of((1 - place[4]) * 32, 32), 32), :].astype(BF16)


def middle_kernel(pieces, keep, received, out):
    running = pieces[0].astype(F32)
    for index in range(1, pieces.shape[0]):
        running = running + pieces[index].astype(F32)
    width = 8 * LANES
    upper = (keep[...] + received[...].astype(F32)).astype(BF16)
    small = running[:, width:].astype(BF16)
    lower = running[:, :width].astype(BF16)
    for far in range(8):
        out[far, :, :width] = lower[4 * far : 4 * far + 4]
        out[far, :, width : 2 * width] = upper[4 * far : 4 * far + 4]
        for group in range(6):
            begin = 2 * width + group * LANES
            out[far, :, begin : begin + LANES] = small[4 * group : 4 * group + 4]


def final_kernel(place, pieces, weight_out, kernel_out, embed_out, *, scale):
    running = pieces[0].astype(F32)
    for index in range(1, pieces.shape[0]):
        running = running + pieces[index].astype(F32)
    running = running * scale
    width = 8 * LANES
    for index in range(8):
        step = STEPS[index % 4]
        core = place[3] if index < 4 else 1 - place[3]
        spot = pl.multiple_of((chip_block(place, step) * 2 + core) * LANES, LANES)
        for layer in range(2):
            begin = layer * width + index * LANES
            weight_out[layer, :, pl.ds(spot, LANES)] = running[:, begin : begin + LANES]

    def small_row(row):
        begin = 2 * width + (row // 4) * LANES
        return running[row % 4 : row % 4 + 1, begin : begin + LANES]

    for index in range(TAPS):
        kernel_out[index, 0:1] = small_row(index)
        kernel_out[index, 1:2] = small_row(TAPS + VOCAB + index)
    for index in range(VOCAB):
        embed_out[index : index + 1] = small_row(TAPS + index)


def spread_kernel(base, grad, before, after, conv, out, wide, *, layer, gap):
    reach = gap * (TAPS // 2)
    wide[:reach] = before[...].astype(F32)
    wide[reach : reach + ROWS] = grad[...].astype(F32)
    wide[reach + ROWS :] = after[...].astype(F32)
    for chunk in range(ROWS // CHUNK):
        row0 = chunk * CHUNK
        running = base[row0 : row0 + CHUNK].astype(F32)
        for index in range(TAPS):
            begin = row0 + (TAPS - 1 - index) * gap
            tap = conv[layer, index : index + 1].astype(F32)
            running = running + tap * wide[begin : begin + CHUNK]
        out[row0 : row0 + CHUNK] = running.astype(BF16)


def spread(base, grad, before, after, conv, layer, gap):
    def kernel(*refs):
        spread_kernel(*refs, layer=layer, gap=gap)

    scratch = [pltpu.VMEM((ROWS + gap * (TAPS - 1), LANES), F32)]
    out = shape((ROWS, LANES), BF16)
    return call(kernel, out, scratch, None, base, grad, before, after, conv)


def seq_shift(cells, step):
    count = lax.axis_size(SEQ)
    if step > 0:
        return lax.ppermute(cells, SEQ, [(i, i + 1) for i in range(count - 1)])
    return lax.ppermute(cells, SEQ, [(i + 1, i) for i in range(count - 1)])


def ring_copies(slab):
    count = lax.axis_size("zh")
    moved = {0: slab}
    for step in (2, 1, 3):
        moved[step] = lax.ppermute(slab, "zh", [(i, (i + step) % count) for i in range(count)])
    return [moved[step] for step in STEPS]


def core_swap(cells):
    return lax.ppermute(cells, "core", [(0, 1), (1, 0)])


def swapped_pairs(mine):
    return core_swap(jnp.stack(mine[:2])), core_swap(jnp.stack(mine[2:]))


def on_device(
    base_ids, span_start, span_length, embedding, conv_kernel, mix_weight, saved_input, cotangent
):
    total_rows = ROWS * lax.axis_size(SEQ)
    place = jnp.stack(
        [
            lax.axis_index(SEQ),
            jnp.int32(total_rows),
            lax.axis_index("zh"),
            lax.axis_index("core"),
            lax.axis_index("zl"),
        ]
    ).astype(jnp.int32)
    smem = pl.BlockSpec(memory_space=pltpu.SMEM)
    vmem = pl.BlockSpec(memory_space=pltpu.VMEM)
    ids = base_ids.reshape(ROWS // 128, 128)
    slab = shape((ROWS, LANES), BF16)
    slab_wide = shape((ROWS, LANES), F32)
    turned = shape((LANES, ROWS), BF16)

    message = shape((MESSAGE, LANES), BF16)
    to_next, to_prev = call_staged(
        pack_kernel, (message, message), [], None, saved_input, ids
    )
    before = seq_shift(to_next, 1)
    after = seq_shift(to_prev, -1)
    mine = ring_copies(cotangent)

    slope_up, act_up, slope_low, act_low, masked, hot = call_staged(
        prep_kernel,
        (slab_wide, turned, slab_wide, turned, slab, shape((128, ROWS), BF16)),
        [
            pltpu.VMEM((ROWS + 2 * CHUNK, 128), F32),
            pltpu.VMEM((ROWS + 2 * LOW_REACH, 128), F32),
            pltpu.VMEM((ROWS + 2 * HIGH_REACH, LANES), F32),
            pltpu.VMEM((ROWS + 2 * LOW_REACH, LANES), F32),
            pltpu.VMEM((128, LANES), F32),
            pltpu.VMEM((ROWS, LANES), BF16),
        ],
        place, before, after, saved_input, cotangent, ids,
        span_start.reshape(-1, 128), span_length.reshape(-1, 128), embedding, conv_kernel,
    )
    slope_up, mine[1], mine[2], mine[3] = lax.optimization_barrier(
        (slope_up, mine[1], mine[2], mine[3])
    )
    pairs = swapped_pairs(mine)

    weight_specs = [
        pl.BlockSpec((1, LANES, 8 * LANES), lambda step: (0, 0, 0)),
        pl.BlockSpec((1, LANES, 8 * LANES), lambda step: (1, 0, 0)),
    ]
    rim = shape((HIGH_REACH, LANES), BF16)
    grad_upper, head, tail = call(
        upper_kernel,
        (slab, rim, rim),
        [],
        [smem] + [vmem] * 6 + [weight_specs[1], vmem],
        place, *mine, *pairs, mix_weight, slope_up,
    )
    up_before = seq_shift(tail, 1)
    up_after = seq_shift(head, -1)
    up_mid = spread(masked, grad_upper, up_before, up_after, conv_kernel, 1, HIGH_GAP)
    mid = ring_copies(up_mid)
    mid_pairs = swapped_pairs(mid)

    far_specs = (pl.BlockSpec(memory_space=pltpu.HBM), vmem)
    upper_outer, upper_taps = call(
        upper_outer_kernel,
        (pltpu.HBM((LANES, 8 * LANES), BF16), shape((16, LANES), F32)),
        [
            pltpu.VMEM((ROWS + 2 * HIGH_REACH, LANES), F32),
            pltpu.VMEM((LANES, 8 * LANES), BF16),
            pltpu.SemaphoreType.DMA((8,)),
        ],
        [vmem] * 11,
        act_up, *mine, *pairs, grad_upper, before, saved_input, after, out_specs=far_specs,
    )
    pieces = lax.all_to_all(upper_outer.reshape(4, 64, 8 * LANES), "x", 0, 0)
    keep, send = call(
        upper_half_kernel,
        (shape((32, 8 * LANES), F32), shape((32, 8 * LANES), BF16)),
        [pltpu.VMEM((64, 8 * LANES), F32)],
        [smem, vmem],
        place, pieces,
    )
    received = lax.ppermute(send, "zl", [(0, 1), (1, 0)])

    lower_outer, grad_lower = call(
        lower_kernel,
        (pltpu.HBM((LANES, 9 * LANES), BF16), slab),
        [
            pltpu.VMEM((32, LANES), F32),
            pltpu.VMEM((8, LANES), F32),
            pltpu.VMEM((LANES, 9 * LANES), BF16),
            pltpu.SemaphoreType.DMA((9,)),
        ],
        [smem] + [vmem] * 7 + [weight_specs[0]] + [vmem] * 6,
        place, act_low, *mid, *mid_pairs, mix_weight, slope_low, hot, up_mid, embedding,
        conv_kernel, upper_taps, out_specs=far_specs,
    )
    pieces = lax.all_to_all(lower_outer.reshape(8, 32, 9 * LANES), NEAR, 0, 0)
    low_before = seq_shift(grad_lower[ROWS - LOW_REACH :], 1)
    low_after = seq_shift(grad_lower[:LOW_REACH], -1)
    input_grad = spread(up_mid, grad_lower, low_before, low_after, conv_kernel, 0, LOW_GAP)
    middle = call(
        middle_kernel, shape((8, 4, 22 * LANES), BF16), [], None, pieces, keep, received
    )
    pieces = lax.all_to_all(middle, "y", 0, 0)

    def finish(*refs):
        final_kernel(*refs, scale=1.0 / math.sqrt(total_rows))

    weight_grad, kernel_grad, embed_grad = call(
        finish,
        (shape((2, 4, 8 * LANES), F32), shape((TAPS, 2, LANES), F32), shape((VOCAB, LANES), F32)),
        [],
        [smem, vmem],
        place, pieces,
    )
    return (input_grad, weight_grad, kernel_grad.transpose(1, 0, 2), embed_grad)


def solution(mesh):
    fine = Mesh(mesh.devices.reshape(8, 2, 4, 4, 2), SEQ + BLK)
    placed = (
        P(SEQ),
        P(),
        P(),
        P(None, BLK),
        P(None, None, BLK),
        P(None, BLK, None),
        P(SEQ, BLK),
        P(SEQ, BLK),
    )
    return jax.shard_map(
        on_device,
        mesh=fine,
        in_specs=placed,
        out_specs=(
            P(SEQ, BLK),
            P(None, BLK + SEQ, None),
            P(None, None, BLK),
            P(None, BLK),
        ),
        check_vma=False,
    )
```

```python
import math

import jax
import jax.numpy as jnp
from jax import lax
from jax.experimental import pallas as pl
from jax.experimental.pallas import tpu as pltpu
from jax.sharding import Mesh, PartitionSpec as P

BASE_DILATION = 4

SEQ = ("y", "zl", "x")
BLK = ("zh", "core")
NEAR = ("zl", "x")
STEPS = (0, 1, 3, 2)

mask_token = 4
gelu_scale = 0.7978845608028654
gelu_cubic = 0.044715
LANES = 256
BF16 = jnp.bfloat16
F32 = jnp.float32

ROWS = 512
TAPS = 9
VOCAB = 5
LOW_GAP, HIGH_GAP = BASE_DILATION, 2 * BASE_DILATION
LOW_REACH, HIGH_REACH = 4 * LOW_GAP, 4 * HIGH_GAP
EDGE = HIGH_REACH
MESSAGE = EDGE + 16
CHUNK = 64
LOWER_COST = 10000000000
PAIRED = (((1,), (1,)), ((), ()))


def gelu_pair(pre_act):
    square = pre_act * pre_act
    tangent = jnp.tanh(gelu_scale * (pre_act + gelu_cubic * square * pre_act))
    half = 0.5 * (1.0 + tangent)
    derivative = half + 0.5 * pre_act * (1.0 - tangent * tangent) * gelu_scale * (
        1.0 + 3.0 * gelu_cubic * square
    )
    return (pre_act * half, derivative)


def call(kernel, outs, scratch, in_specs, *operands, out_specs=None, cost=None):
    extra = {} if in_specs is None else {"in_specs": in_specs, "grid": (1,)}
    if cost is not None:
        extra["cost_estimate"] = pl.CostEstimate(
            flops=cost, transcendentals=0, bytes_accessed=0
        )
    if out_specs is not None:
        extra["out_specs"] = out_specs
    return pl.pallas_call(
        kernel,
        out_shape=outs,
        scratch_shapes=scratch,
        compiler_params=pltpu.CompilerParams(vmem_limit_bytes=16 << 20),
        **extra,
    )(*operands)


def call_staged(kernel, outs, scratch, place, *operands):
    count = len(operands)
    lead = 0 if place is None else 1

    def staged(*refs):
        head, sources, rest = refs[:lead], refs[lead : lead + count], refs[lead + count :]
        held, sems = rest[-count - 1 : -1], rest[-1]
        loads = [
            pltpu.make_async_copy(sources[index], held[index], sems.at[index])
            for index in range(count)
        ]
        for load in loads:
            load.start()
        for load in loads:
            load.wait()
        kernel(*head, *held, *rest[: -count - 1])

    smem = pl.BlockSpec(memory_space=pltpu.SMEM)
    hbm = pl.BlockSpec(memory_space=pltpu.HBM)
    operands = [pltpu.with_memory_space_constraint(cells, pltpu.HBM) for cells in operands]
    return pl.pallas_call(
        staged,
        out_shape=outs,
        in_specs=[smem] * lead + [hbm] * count,
        scratch_shapes=list(scratch)
        + [pltpu.VMEM(cells.shape, cells.dtype) for cells in operands]
        + [pltpu.SemaphoreType.DMA((count,))],
        compiler_params=pltpu.CompilerParams(vmem_limit_bytes=24 << 20),
    )(*(() if place is None else (place,)), *operands)


def shape(dims, kind):
    return jax.ShapeDtypeStruct(dims, kind)


def pack_kernel(saved, ids, next_out, prev_out):
    for out, begin, row in ((next_out, ROWS - EDGE, 3), (prev_out, 0, 0)):
        out[:EDGE] = saved[begin : begin + EDGE]
        line = jnp.broadcast_to(ids[row : row + 1].astype(F32), (MESSAGE - EDGE, 128))
        out[EDGE:] = jnp.concatenate([line, line], axis=1).astype(BF16)


def prep_kernel(
    place, before, after, saved, cot, ids, start, length, embedding, conv,
    slope_up, act_up, slope_low, act_low, masked, hot_out,
    cover, idw, wide, first, table, act_all,
):
    base = place[0] * ROWS - CHUNK
    total = place[1]

    def cover_chunk(index, carry):
        row0 = pl.multiple_of(index * CHUNK, CHUNK)
        here = lax.broadcasted_iota(jnp.int32, (CHUNK, 128), 0) + (base + row0)
        hit = jnp.zeros((CHUNK, 128), jnp.int32)
        for group in range(start.shape[0]):
            gap = here - start[group : group + 1]
            hit = jnp.where((gap >= 0) & (gap < length[group : group + 1]), 1, hit)
        seen = jnp.max(hit, axis=1, keepdims=True).astype(F32)
        cover[pl.ds(row0, CHUNK), :] = jnp.broadcast_to(seen, (CHUNK, 128))
        return carry

    lax.fori_loop(0, ROWS // CHUNK + 2, cover_chunk, 0)

    def column(row):
        return jnp.transpose(jnp.broadcast_to(row.astype(F32), (128, 128)))

    idw[:LOW_REACH] = column(before[EDGE : EDGE + 1, :128])[128 - LOW_REACH :]
    for piece in range(ROWS // 128):
        idw[LOW_REACH + 128 * piece : LOW_REACH + 128 * (piece + 1)] = column(ids[piece : piece + 1])
    idw[LOW_REACH + ROWS :] = column(after[EDGE : EDGE + 1, :128])[:LOW_REACH]
    spread = ROWS + 2 * LOW_REACH
    spot = lax.broadcasted_iota(jnp.int32, (spread, 128), 0) + (base + CHUNK - LOW_REACH)
    lane = lax.broadcasted_iota(jnp.int32, (1, 128), 1)
    tokens = jnp.where(
        cover[CHUNK - LOW_REACH : CHUNK - LOW_REACH + spread] > 0.0,
        float(mask_token),
        idw[...],
    )
    tokens = jnp.where((spot >= 0) & (spot < total), tokens, 7.0)
    idw[...] = tokens
    table[...] = jnp.zeros_like(table)
    table[:VOCAB] = embedding[...].astype(F32)
    hot = jnp.where(tokens == lane.astype(F32), 1.0, 0.0).astype(BF16)
    first[...] = jnp.dot(hot, table[...].astype(BF16), preferred_element_type=F32)

    channel = lax.broadcasted_iota(jnp.int32, (LANES, LANES), 1)
    target = lax.broadcasted_iota(jnp.int32, (LANES, LANES), 0)
    tail = ((channel >> 5) << 2) | (channel & 3)
    low_place = (((channel >> 2) & 7) << 5) | tail
    low_shuffle = jnp.where(low_place == target, 1.0, 0.0).astype(BF16)

    taps_low = [conv[0, index : index + 1].astype(F32) for index in range(TAPS)]
    for chunk in range(ROWS // CHUNK):
        row0 = chunk * CHUNK
        pre = None
        for index in range(TAPS):
            begin = row0 + index * LOW_GAP
            term = taps_low[index] * first[begin : begin + CHUNK]
            pre = term if pre is None else pre + term
        act, slope = gelu_pair(pre)
        slope_low[row0 : row0 + CHUNK] = slope
        act_all[row0 : row0 + CHUNK] = act.astype(BF16)
    act_low[...] = lax.dot_general(
        low_shuffle, act_all[:ROWS], PAIRED, preferred_element_type=F32
    ).astype(BF16)

    picked = idw[:ROWS]
    for index in range(1, TAPS):
        picked = jnp.where((lane >> 3) == index, idw[index * LOW_GAP : index * LOW_GAP + ROWS], picked)
    kind = lane & 7
    live = (kind < VOCAB) & (lane < 8 * TAPS)
    hot = jnp.where((picked == kind.astype(F32)) & live, 1.0, 0.0)
    hot_out[...] = jnp.transpose(hot).astype(BF16)

    wide[:HIGH_REACH] = before[:HIGH_REACH].astype(F32)
    wide[HIGH_REACH : HIGH_REACH + ROWS] = saved[...].astype(F32)
    wide[HIGH_REACH + ROWS :] = after[:HIGH_REACH].astype(F32)
    taps_up = [conv[1, index : index + 1].astype(F32) for index in range(TAPS)]
    for chunk in range(ROWS // CHUNK):
        row0 = chunk * CHUNK
        pre = None
        for index in range(TAPS):
            begin = row0 + index * HIGH_GAP
            term = taps_up[index] * wide[begin : begin + CHUNK]
            pre = term if pre is None else pre + term
        act, slope = gelu_pair(pre)
        seen = cover[CHUNK + row0 : 2 * CHUNK + row0] > 0.0
        seen = jnp.concatenate([seen, seen], axis=1)
        slope_up[row0 : row0 + CHUNK] = jnp.where(seen, slope, 0.0)
        act_all[row0 : row0 + CHUNK] = jnp.where(seen, act, 0.0).astype(BF16)
        masked[row0 : row0 + CHUNK] = jnp.where(
            seen, cot[row0 : row0 + CHUNK].astype(F32), 0.0
        ).astype(BF16)
    act_up[...] = lax.dot_general(
        low_shuffle, act_all[:ROWS], PAIRED, preferred_element_type=F32
    ).astype(BF16)


def chip_block(place, step):
    return (place[2] - step) & 3


def weight_columns(weights, place, step, core):
    block = chip_block(place, step) * 2 + core
    return weights[0, :, pl.ds(pl.multiple_of(block * LANES, LANES), LANES)]


def product_over_blocks(place, mine, pairs, weights):
    total = None
    for index, step in enumerate(STEPS):
        term = lax.dot_general(
            mine[index][...], weight_columns(weights, place, step, place[3]), PAIRED,
            preferred_element_type=F32,
        )
        total = term if total is None else total + term
    for index, step in enumerate(STEPS):
        total = total + lax.dot_general(
            pairs[index // 2][index % 2], weight_columns(weights, place, step, 1 - place[3]),
            PAIRED, preferred_element_type=F32,
        )
    return total


def upper_kernel(place, m0, m1, m2, m3, p0, p1, weights, slope, grad_out, head_out, tail_out):
    grad = product_over_blocks(place, (m0, m1, m2, m3), (p0, p1), weights) * slope[...]
    grad = grad.astype(BF16)
    grad_out[...] = grad
    head_out[...] = grad[:HIGH_REACH]
    tail_out[...] = grad[ROWS - HIGH_REACH :]


def outer_product(act, mine, pairs, out, stage, sems):
    copies = []
    for index in range(2 * len(STEPS)):
        half = index % len(STEPS)
        piece = mine[half][...] if index < len(STEPS) else pairs[half // 2][half % 2]
        lanes = slice(index * LANES, (index + 1) * LANES)
        stage[:, lanes] = jnp.dot(act[...], piece, preferred_element_type=F32).astype(BF16)
        copies.append(
            pltpu.make_async_copy(stage.at[:, lanes], out.at[:, lanes], sems.at[index])
        )
        copies[-1].start()
    return copies


def upper_outer_kernel(
    act, m0, m1, m2, m3, p0, p1, grad, before, saved, after, out, tap_out, wide, stage, sems
):
    copies = outer_product(act, (m0, m1, m2, m3), (p0, p1), out, stage, sems)
    wide[:HIGH_REACH] = before[:HIGH_REACH].astype(F32)
    wide[HIGH_REACH : HIGH_REACH + ROWS] = saved[...].astype(F32)
    wide[HIGH_REACH + ROWS :] = after[:HIGH_REACH].astype(F32)
    sums = [jnp.zeros((8, LANES), F32) for index in range(TAPS)]
    for chunk in range(ROWS // CHUNK):
        row0 = chunk * CHUNK
        grad_wide = grad[row0 : row0 + CHUNK].astype(F32)
        for index in range(TAPS):
            begin = row0 + index * HIGH_GAP
            term = grad_wide * wide[begin : begin + CHUNK]
            sums[index] = sums[index] + jnp.sum(term.reshape(CHUNK // 8, 8, LANES), axis=0)
    tap_out[...] = jnp.zeros_like(tap_out)
    for index in range(TAPS):
        tap_out[index : index + 1] = jnp.sum(sums[index], axis=0, keepdims=True)
    for copy in copies:
        copy.wait()


def lower_kernel(
    place, act, m0, m1, m2, m3, p0, p1, weights, slope, hot, up_row, embedding, conv, upper_taps,
    out, grad_out, small, table, stage, sems,
):
    mine, pairs = (m0, m1, m2, m3), (p0, p1)
    grad = (product_over_blocks(place, mine, pairs, weights) * slope[...]).astype(BF16)
    grad_out[...] = grad
    copies = outer_product(act, mine, pairs, out, stage, sems)
    picked = jnp.dot(hot[...], grad, preferred_element_type=F32)
    embed = jnp.dot(hot[32:48], up_row[...], preferred_element_type=F32)[:8]
    table[...] = jnp.zeros_like(table)
    table[:VOCAB] = embedding[...].astype(F32)
    small[...] = jnp.zeros_like(small)
    for index in range(TAPS):
        piece = picked[index * 8 : index * 8 + 8]
        small[index : index + 1] = jnp.sum(piece * table[...], axis=0, keepdims=True)
        embed = embed + piece * conv[0, index : index + 1].astype(F32)
    small[TAPS : TAPS + VOCAB] = embed[:VOCAB]
    small[TAPS + VOCAB : 2 * TAPS + VOCAB] = upper_taps[:TAPS]
    packed = small[...].astype(BF16)
    for index in range(LANES // 32):
        stage[index * 32 : (index + 1) * 32, 8 * LANES :] = packed
    last = pltpu.make_async_copy(
        stage.at[:, 8 * LANES :], out.at[:, 8 * LANES :], sems.at[8]
    )
    last.start()
    for copy in copies + [last]:
        copy.wait()


def add_up(pieces):
    running = pieces[0].astype(F32)
    for index in range(1, pieces.shape[0]):
        running = running + pieces[index].astype(F32)
    return running


def upper_sum_kernel(pieces, out):
    out[...] = add_up(pieces).astype(BF16)


def middle_kernel(pieces, upper, out):
    running = pieces[0].astype(F32)
    for index in range(1, pieces.shape[0]):
        running = running + pieces[index].astype(F32)
    width = 8 * LANES
    upper = upper[...]
    small = running[:, width:].astype(BF16)
    lower = running[:, :width].astype(BF16)
    for far in range(8):
        out[far, :, :width] = lower[4 * far : 4 * far + 4]
        out[far, :, width : 2 * width] = upper[4 * far : 4 * far + 4]
        for group in range(6):
            begin = 2 * width + group * LANES
            out[far, :, begin : begin + LANES] = small[4 * group : 4 * group + 4]


def final_kernel(place, pieces, weight_out, kernel_out, embed_out, *, scale):
    running = pieces[0].astype(F32)
    for index in range(1, pieces.shape[0]):
        running = running + pieces[index].astype(F32)
    running = running * scale
    width = 8 * LANES
    for index in range(8):
        step = STEPS[index % 4]
        core = place[3] if index < 4 else 1 - place[3]
        spot = pl.multiple_of((chip_block(place, step) * 2 + core) * LANES, LANES)
        for layer in range(2):
            begin = layer * width + index * LANES
            weight_out[layer, :, pl.ds(spot, LANES)] = running[:, begin : begin + LANES]

    def small_row(row):
        begin = 2 * width + (row // 4) * LANES
        return running[row % 4 : row % 4 + 1, begin : begin + LANES]

    for index in range(TAPS):
        kernel_out[index, 0:1] = small_row(index)
        kernel_out[index, 1:2] = small_row(TAPS + VOCAB + index)
    for index in range(VOCAB):
        embed_out[index : index + 1] = small_row(TAPS + index)


def spread_kernel(base, grad, before, after, conv, out, wide, *, layer, gap):
    reach = gap * (TAPS // 2)
    wide[:reach] = before[...].astype(F32)
    wide[reach : reach + ROWS] = grad[...].astype(F32)
    wide[reach + ROWS :] = after[...].astype(F32)
    for chunk in range(ROWS // CHUNK):
        row0 = chunk * CHUNK
        running = base[row0 : row0 + CHUNK].astype(F32)
        for index in range(TAPS):
            begin = row0 + (TAPS - 1 - index) * gap
            tap = conv[layer, index : index + 1].astype(F32)
            running = running + tap * wide[begin : begin + CHUNK]
        out[row0 : row0 + CHUNK] = running.astype(BF16)


def spread(base, grad, before, after, conv, layer, gap):
    def kernel(*refs):
        spread_kernel(*refs, layer=layer, gap=gap)

    scratch = [pltpu.VMEM((ROWS + gap * (TAPS - 1), LANES), F32)]
    out = shape((ROWS, LANES), BF16)
    return call(kernel, out, scratch, None, base, grad, before, after, conv)


def seq_shift(cells, step):
    count = lax.axis_size(SEQ)
    if step > 0:
        return lax.ppermute(cells, SEQ, [(i, i + 1) for i in range(count - 1)])
    return lax.ppermute(cells, SEQ, [(i + 1, i) for i in range(count - 1)])


def ring_copies(slab):
    count = lax.axis_size("zh")
    moved = {0: slab}
    for step in (2, 1, 3):
        moved[step] = lax.ppermute(slab, "zh", [(i, (i + step) % count) for i in range(count)])
    return [moved[step] for step in STEPS]


def core_swap(cells):
    return lax.ppermute(cells, "core", [(0, 1), (1, 0)])


def swapped_pairs(mine):
    return core_swap(jnp.stack(mine[:2])), core_swap(jnp.stack(mine[2:]))


def on_device(
    base_ids, span_start, span_length, embedding, conv_kernel, mix_weight, saved_input, cotangent
):
    total_rows = ROWS * lax.axis_size(SEQ)
    place = jnp.stack(
        [
            lax.axis_index(SEQ),
            jnp.int32(total_rows),
            lax.axis_index("zh"),
            lax.axis_index("core"),
            lax.axis_index("zl"),
        ]
    ).astype(jnp.int32)
    smem = pl.BlockSpec(memory_space=pltpu.SMEM)
    vmem = pl.BlockSpec(memory_space=pltpu.VMEM)
    ids = base_ids.reshape(ROWS // 128, 128)
    slab = shape((ROWS, LANES), BF16)
    slab_wide = shape((ROWS, LANES), F32)
    turned = shape((LANES, ROWS), BF16)

    message = shape((MESSAGE, LANES), BF16)
    to_next, to_prev = call_staged(
        pack_kernel, (message, message), [], None, saved_input, ids
    )
    before = seq_shift(to_next, 1)
    after = seq_shift(to_prev, -1)
    mine = ring_copies(cotangent)

    slope_up, act_up, slope_low, act_low, masked, hot = call_staged(
        prep_kernel,
        (slab_wide, turned, slab_wide, turned, slab, shape((128, ROWS), BF16)),
        [
            pltpu.VMEM((ROWS + 2 * CHUNK, 128), F32),
            pltpu.VMEM((ROWS + 2 * LOW_REACH, 128), F32),
            pltpu.VMEM((ROWS + 2 * HIGH_REACH, LANES), F32),
            pltpu.VMEM((ROWS + 2 * LOW_REACH, LANES), F32),
            pltpu.VMEM((128, LANES), F32),
            pltpu.VMEM((ROWS, LANES), BF16),
        ],
        place, before, after, saved_input, cotangent, ids,
        span_start.reshape(-1, 128), span_length.reshape(-1, 128), embedding, conv_kernel,
    )
    slope_up, mine[1], mine[2], mine[3] = lax.optimization_barrier(
        (slope_up, mine[1], mine[2], mine[3])
    )
    pairs = swapped_pairs(mine)

    weight_specs = [
        pl.BlockSpec((1, LANES, 8 * LANES), lambda step: (0, 0, 0)),
        pl.BlockSpec((1, LANES, 8 * LANES), lambda step: (1, 0, 0)),
    ]
    rim = shape((HIGH_REACH, LANES), BF16)
    grad_upper, head, tail = call(
        upper_kernel,
        (slab, rim, rim),
        [],
        [smem] + [vmem] * 6 + [weight_specs[1], vmem],
        place, *mine, *pairs, mix_weight, slope_up,
    )
    up_before = seq_shift(tail, 1)
    up_after = seq_shift(head, -1)
    up_mid = spread(masked, grad_upper, up_before, up_after, conv_kernel, 1, HIGH_GAP)
    mid = ring_copies(up_mid)
    mid_pairs = swapped_pairs(mid)

    far_specs = (pl.BlockSpec(memory_space=pltpu.HBM), vmem)
    upper_outer, upper_taps = call(
        upper_outer_kernel,
        (pltpu.HBM((LANES, 8 * LANES), BF16), shape((16, LANES), F32)),
        [
            pltpu.VMEM((ROWS + 2 * HIGH_REACH, LANES), F32),
            pltpu.VMEM((LANES, 8 * LANES), BF16),
            pltpu.SemaphoreType.DMA((8,)),
        ],
        [vmem] * 11,
        act_up, *mine, *pairs, grad_upper, before, saved_input, after, out_specs=far_specs,
    )
    pieces = lax.all_to_all(upper_outer.reshape(8, 32, 8 * LANES), NEAR, 0, 0)
    upper_sum = call(upper_sum_kernel, shape((32, 8 * LANES), BF16), [], None, pieces)

    lower_outer, grad_lower = call(
        lower_kernel,
        (pltpu.HBM((LANES, 9 * LANES), BF16), slab),
        [
            pltpu.VMEM((32, LANES), F32),
            pltpu.VMEM((8, LANES), F32),
            pltpu.VMEM((LANES, 9 * LANES), BF16),
            pltpu.SemaphoreType.DMA((9,)),
        ],
        [smem] + [vmem] * 7 + [weight_specs[0]] + [vmem] * 6,
        place, act_low, *mid, *mid_pairs, mix_weight, slope_low, hot, up_mid, embedding,
        conv_kernel, upper_taps, out_specs=far_specs, cost=LOWER_COST,
    )
    pieces = lax.all_to_all(lower_outer.reshape(8, 32, 9 * LANES), NEAR, 0, 0)
    low_before = seq_shift(grad_lower[ROWS - LOW_REACH :], 1)
    low_after = seq_shift(grad_lower[:LOW_REACH], -1)
    input_grad = spread(up_mid, grad_lower, low_before, low_after, conv_kernel, 0, LOW_GAP)
    middle = call(
        middle_kernel, shape((8, 4, 22 * LANES), BF16), [], None, pieces, upper_sum
    )
    pieces = lax.all_to_all(middle, "y", 0, 0)

    def finish(*refs):
        final_kernel(*refs, scale=1.0 / math.sqrt(total_rows))

    weight_grad, kernel_grad, embed_grad = call(
        finish,
        (shape((2, 4, 8 * LANES), F32), shape((TAPS, 2, LANES), F32), shape((VOCAB, LANES), F32)),
        [],
        [smem, vmem],
        place, pieces,
    )
    return (input_grad, weight_grad, kernel_grad.transpose(1, 0, 2), embed_grad)


def solution(mesh):
    fine = Mesh(mesh.devices.reshape(8, 2, 4, 4, 2), SEQ + BLK)
    placed = (
        P(SEQ),
        P(),
        P(),
        P(None, BLK),
        P(None, None, BLK),
        P(None, BLK, None),
        P(SEQ, BLK),
        P(SEQ, BLK),
    )
    return jax.shard_map(
        on_device,
        mesh=fine,
        in_specs=placed,
        out_specs=(
            P(SEQ, BLK),
            P(None, BLK + SEQ, None),
            P(None, None, BLK),
            P(None, BLK),
        ),
        check_vma=False,
    )
```

```python
import math

import jax
import jax.numpy as jnp
from jax import lax
from jax.experimental import pallas as pl
from jax.experimental.pallas import tpu as pltpu
from jax.sharding import Mesh, PartitionSpec as P

BASE_DILATION = 4

SEQ = ("y", "zl", "x")
BLK = ("zh", "core")
NEAR = ("zl", "x")
STEPS = (0, 1, 3, 2)

mask_token = 4
gelu_scale = 0.7978845608028654
gelu_cubic = 0.044715
LANES = 256
BF16 = jnp.bfloat16
F32 = jnp.float32

ROWS = 512
TAPS = 9
VOCAB = 5
LOW_GAP, HIGH_GAP = BASE_DILATION, 2 * BASE_DILATION
LOW_REACH, HIGH_REACH = 4 * LOW_GAP, 4 * HIGH_GAP
EDGE = HIGH_REACH
MESSAGE = EDGE + 16
CHUNK = 64
LOWER_COST = 10000000000
PAIRED = (((1,), (1,)), ((), ()))


def gelu_pair(pre_act):
    square = pre_act * pre_act
    tangent = jnp.tanh(gelu_scale * (pre_act + gelu_cubic * square * pre_act))
    half = 0.5 * (1.0 + tangent)
    derivative = half + 0.5 * pre_act * (1.0 - tangent * tangent) * gelu_scale * (
        1.0 + 3.0 * gelu_cubic * square
    )
    return (pre_act * half, derivative)


def call(kernel, outs, scratch, in_specs, *operands, out_specs=None, cost=None):
    extra = {} if in_specs is None else {"in_specs": in_specs, "grid": (1,)}
    if cost is not None:
        extra["cost_estimate"] = pl.CostEstimate(
            flops=cost, transcendentals=0, bytes_accessed=0
        )
    if out_specs is not None:
        extra["out_specs"] = out_specs
    return pl.pallas_call(
        kernel,
        out_shape=outs,
        scratch_shapes=scratch,
        compiler_params=pltpu.CompilerParams(vmem_limit_bytes=16 << 20),
        **extra,
    )(*operands)


def call_staged(kernel, outs, scratch, place, *operands):
    count = len(operands)
    lead = 0 if place is None else 1

    def staged(*refs):
        head, sources, rest = refs[:lead], refs[lead : lead + count], refs[lead + count :]
        held, sems = rest[-count - 1 : -1], rest[-1]
        loads = [
            pltpu.make_async_copy(sources[index], held[index], sems.at[index])
            for index in range(count)
        ]
        for load in loads:
            load.start()
        for load in loads:
            load.wait()
        kernel(*head, *held, *rest[: -count - 1])

    smem = pl.BlockSpec(memory_space=pltpu.SMEM)
    hbm = pl.BlockSpec(memory_space=pltpu.HBM)
    operands = [pltpu.with_memory_space_constraint(cells, pltpu.HBM) for cells in operands]
    return pl.pallas_call(
        staged,
        out_shape=outs,
        in_specs=[smem] * lead + [hbm] * count,
        scratch_shapes=list(scratch)
        + [pltpu.VMEM(cells.shape, cells.dtype) for cells in operands]
        + [pltpu.SemaphoreType.DMA((count,))],
        compiler_params=pltpu.CompilerParams(vmem_limit_bytes=24 << 20),
    )(*(() if place is None else (place,)), *operands)


def shape(dims, kind):
    return jax.ShapeDtypeStruct(dims, kind)


def pack_kernel(saved, ids, next_out, prev_out):
    for out, begin, row in ((next_out, ROWS - EDGE, 3), (prev_out, 0, 0)):
        out[:EDGE] = saved[begin : begin + EDGE]
        line = jnp.broadcast_to(ids[row : row + 1].astype(F32), (MESSAGE - EDGE, 128))
        out[EDGE:] = jnp.concatenate([line, line], axis=1).astype(BF16)


def prep_kernel(
    place, before, after, saved, cot, ids, start, length, embedding, conv,
    slope_up, act_up, slope_low, act_low, masked, hot_out,
    cover, idw, wide, first, table, act_all,
):
    base = place[0] * ROWS - CHUNK
    total = place[1]

    def cover_chunk(index, carry):
        row0 = pl.multiple_of(index * CHUNK, CHUNK)
        here = lax.broadcasted_iota(jnp.int32, (CHUNK, 128), 0) + (base + row0)
        hit = jnp.zeros((CHUNK, 128), jnp.int32)
        for group in range(start.shape[0]):
            gap = here - start[group : group + 1]
            hit = jnp.where((gap >= 0) & (gap < length[group : group + 1]), 1, hit)
        seen = jnp.max(hit, axis=1, keepdims=True).astype(F32)
        cover[pl.ds(row0, CHUNK), :] = jnp.broadcast_to(seen, (CHUNK, 128))
        return carry

    lax.fori_loop(0, ROWS // CHUNK + 2, cover_chunk, 0)

    def column(row):
        return jnp.transpose(jnp.broadcast_to(row.astype(F32), (128, 128)))

    idw[:LOW_REACH] = column(before[EDGE : EDGE + 1, :128])[128 - LOW_REACH :]
    for piece in range(ROWS // 128):
        idw[LOW_REACH + 128 * piece : LOW_REACH + 128 * (piece + 1)] = column(ids[piece : piece + 1])
    idw[LOW_REACH + ROWS :] = column(after[EDGE : EDGE + 1, :128])[:LOW_REACH]
    spread = ROWS + 2 * LOW_REACH
    spot = lax.broadcasted_iota(jnp.int32, (spread, 128), 0) + (base + CHUNK - LOW_REACH)
    lane = lax.broadcasted_iota(jnp.int32, (1, 128), 1)
    tokens = jnp.where(
        cover[CHUNK - LOW_REACH : CHUNK - LOW_REACH + spread] > 0.0,
        float(mask_token),
        idw[...],
    )
    tokens = jnp.where((spot >= 0) & (spot < total), tokens, 7.0)
    idw[...] = tokens
    table[...] = jnp.zeros_like(table)
    table[:VOCAB] = embedding[...].astype(F32)
    hot = jnp.where(tokens == lane.astype(F32), 1.0, 0.0).astype(BF16)
    first[...] = jnp.dot(hot, table[...].astype(BF16), preferred_element_type=F32)

    channel = lax.broadcasted_iota(jnp.int32, (LANES, LANES), 1)
    target = lax.broadcasted_iota(jnp.int32, (LANES, LANES), 0)
    tail = ((channel >> 5) << 2) | (channel & 3)
    low_place = (((channel >> 2) & 7) << 5) | tail
    low_shuffle = jnp.where(low_place == target, 1.0, 0.0).astype(BF16)

    taps_low = [conv[0, index : index + 1].astype(F32) for index in range(TAPS)]
    for chunk in range(ROWS // CHUNK):
        row0 = chunk * CHUNK
        pre = None
        for index in range(TAPS):
            begin = row0 + index * LOW_GAP
            term = taps_low[index] * first[begin : begin + CHUNK]
            pre = term if pre is None else pre + term
        act, slope = gelu_pair(pre)
        slope_low[row0 : row0 + CHUNK] = slope
        act_all[row0 : row0 + CHUNK] = act.astype(BF16)
    act_low[...] = lax.dot_general(
        low_shuffle, act_all[:ROWS], PAIRED, preferred_element_type=F32
    ).astype(BF16)

    picked = idw[:ROWS]
    for index in range(1, TAPS):
        picked = jnp.where((lane >> 3) == index, idw[index * LOW_GAP : index * LOW_GAP + ROWS], picked)
    kind = lane & 7
    live = (kind < VOCAB) & (lane < 8 * TAPS)
    hot = jnp.where((picked == kind.astype(F32)) & live, 1.0, 0.0)
    hot_out[...] = jnp.transpose(hot).astype(BF16)

    wide[:HIGH_REACH] = before[:HIGH_REACH].astype(F32)
    wide[HIGH_REACH : HIGH_REACH + ROWS] = saved[...].astype(F32)
    wide[HIGH_REACH + ROWS :] = after[:HIGH_REACH].astype(F32)
    taps_up = [conv[1, index : index + 1].astype(F32) for index in range(TAPS)]
    for chunk in range(ROWS // CHUNK):
        row0 = chunk * CHUNK
        pre = None
        for index in range(TAPS):
            begin = row0 + index * HIGH_GAP
            term = taps_up[index] * wide[begin : begin + CHUNK]
            pre = term if pre is None else pre + term
        act, slope = gelu_pair(pre)
        seen = cover[CHUNK + row0 : 2 * CHUNK + row0] > 0.0
        seen = jnp.concatenate([seen, seen], axis=1)
        slope_up[row0 : row0 + CHUNK] = jnp.where(seen, slope, 0.0)
        act_all[row0 : row0 + CHUNK] = jnp.where(seen, act, 0.0).astype(BF16)
        masked[row0 : row0 + CHUNK] = jnp.where(
            seen, cot[row0 : row0 + CHUNK].astype(F32), 0.0
        ).astype(BF16)
    act_up[...] = lax.dot_general(
        low_shuffle, act_all[:ROWS], PAIRED, preferred_element_type=F32
    ).astype(BF16)


def swapped(pairs, index):
    lead = 1 if len(pairs[0].shape) == 2 else 2
    if index >= lead:
        return pairs[1][index - lead]
    return pairs[0][...] if lead == 1 else pairs[0][index]


def chip_block(place, step):
    return (place[2] - step) & 3


def weight_columns(weights, place, step, core):
    block = chip_block(place, step) * 2 + core
    return weights[0, :, pl.ds(pl.multiple_of(block * LANES, LANES), LANES)]


def product_over_blocks(place, mine, pairs, weights):
    total = None
    for index, step in enumerate(STEPS):
        term = lax.dot_general(
            mine[index][...], weight_columns(weights, place, step, place[3]), PAIRED,
            preferred_element_type=F32,
        )
        total = term if total is None else total + term
    for index, step in enumerate(STEPS):
        total = total + lax.dot_general(
            swapped(pairs, index), weight_columns(weights, place, step, 1 - place[3]),
            PAIRED, preferred_element_type=F32,
        )
    return total


def upper_kernel(place, m0, m1, m2, m3, p0, p1, weights, slope, grad_out, head_out, tail_out):
    grad = product_over_blocks(place, (m0, m1, m2, m3), (p0, p1), weights) * slope[...]
    grad = grad.astype(BF16)
    grad_out[...] = grad
    head_out[...] = grad[:HIGH_REACH]
    tail_out[...] = grad[ROWS - HIGH_REACH :]


def outer_product(act, mine, pairs, out, stage, sems):
    copies = []
    for index in range(2 * len(STEPS)):
        half = index % len(STEPS)
        piece = mine[half][...] if index < len(STEPS) else swapped(pairs, half)
        lanes = slice(index * LANES, (index + 1) * LANES)
        stage[:, lanes] = jnp.dot(act[...], piece, preferred_element_type=F32).astype(BF16)
        copies.append(
            pltpu.make_async_copy(stage.at[:, lanes], out.at[:, lanes], sems.at[index])
        )
        copies[-1].start()
    return copies


def upper_outer_kernel(
    act, m0, m1, m2, m3, p0, p1, grad, before, saved, after, out, tap_out, wide, stage, sems
):
    copies = outer_product(act, (m0, m1, m2, m3), (p0, p1), out, stage, sems)
    wide[:HIGH_REACH] = before[:HIGH_REACH].astype(F32)
    wide[HIGH_REACH : HIGH_REACH + ROWS] = saved[...].astype(F32)
    wide[HIGH_REACH + ROWS :] = after[:HIGH_REACH].astype(F32)
    sums = [jnp.zeros((8, LANES), F32) for index in range(TAPS)]
    for chunk in range(ROWS // CHUNK):
        row0 = chunk * CHUNK
        grad_wide = grad[row0 : row0 + CHUNK].astype(F32)
        for index in range(TAPS):
            begin = row0 + index * HIGH_GAP
            term = grad_wide * wide[begin : begin + CHUNK]
            sums[index] = sums[index] + jnp.sum(term.reshape(CHUNK // 8, 8, LANES), axis=0)
    tap_out[...] = jnp.zeros_like(tap_out)
    for index in range(TAPS):
        tap_out[index : index + 1] = jnp.sum(sums[index], axis=0, keepdims=True)
    for copy in copies:
        copy.wait()


def lower_kernel(
    place, act, m0, m1, m2, m3, p0, p1, weights, slope, hot, up_row, embedding, conv, upper_taps,
    out, grad_out, small, table, stage, sems,
):
    mine, pairs = (m0, m1, m2, m3), (p0, p1)
    grad = (product_over_blocks(place, mine, pairs, weights) * slope[...]).astype(BF16)
    grad_out[...] = grad
    copies = outer_product(act, mine, pairs, out, stage, sems)
    picked = jnp.dot(hot[...], grad, preferred_element_type=F32)
    embed = jnp.dot(hot[32:48], up_row[...], preferred_element_type=F32)[:8]
    table[...] = jnp.zeros_like(table)
    table[:VOCAB] = embedding[...].astype(F32)
    small[...] = jnp.zeros_like(small)
    for index in range(TAPS):
        piece = picked[index * 8 : index * 8 + 8]
        small[index : index + 1] = jnp.sum(piece * table[...], axis=0, keepdims=True)
        embed = embed + piece * conv[0, index : index + 1].astype(F32)
    small[TAPS : TAPS + VOCAB] = embed[:VOCAB]
    small[TAPS + VOCAB : 2 * TAPS + VOCAB] = upper_taps[:TAPS]
    packed = small[...].astype(BF16)
    for index in range(LANES // 32):
        stage[index * 32 : (index + 1) * 32, 8 * LANES :] = packed
    last = pltpu.make_async_copy(
        stage.at[:, 8 * LANES :], out.at[:, 8 * LANES :], sems.at[8]
    )
    last.start()
    for copy in copies + [last]:
        copy.wait()


def add_up(pieces):
    running = pieces[0].astype(F32)
    for index in range(1, pieces.shape[0]):
        running = running + pieces[index].astype(F32)
    return running


def upper_sum_kernel(pieces, out):
    out[...] = add_up(pieces).astype(BF16)


def middle_kernel(pieces, upper, out):
    running = pieces[0].astype(F32)
    for index in range(1, pieces.shape[0]):
        running = running + pieces[index].astype(F32)
    width = 8 * LANES
    upper = upper[...]
    small = running[:, width:].astype(BF16)
    lower = running[:, :width].astype(BF16)
    for far in range(8):
        out[far, :, :width] = lower[4 * far : 4 * far + 4]
        out[far, :, width : 2 * width] = upper[4 * far : 4 * far + 4]
        for group in range(6):
            begin = 2 * width + group * LANES
            out[far, :, begin : begin + LANES] = small[4 * group : 4 * group + 4]


def final_kernel(place, pieces, weight_out, kernel_out, embed_out, *, scale):
    running = pieces[0].astype(F32)
    for index in range(1, pieces.shape[0]):
        running = running + pieces[index].astype(F32)
    running = running * scale
    width = 8 * LANES
    for index in range(8):
        step = STEPS[index % 4]
        core = place[3] if index < 4 else 1 - place[3]
        spot = pl.multiple_of((chip_block(place, step) * 2 + core) * LANES, LANES)
        for layer in range(2):
            begin = layer * width + index * LANES
            weight_out[layer, :, pl.ds(spot, LANES)] = running[:, begin : begin + LANES]

    def small_row(row):
        begin = 2 * width + (row // 4) * LANES
        return running[row % 4 : row % 4 + 1, begin : begin + LANES]

    for index in range(TAPS):
        kernel_out[index, 0:1] = small_row(index)
        kernel_out[index, 1:2] = small_row(TAPS + VOCAB + index)
    for index in range(VOCAB):
        embed_out[index : index + 1] = small_row(TAPS + index)


def spread_kernel(base, grad, before, after, conv, out, wide, *, layer, gap):
    reach = gap * (TAPS // 2)
    wide[:reach] = before[...].astype(F32)
    wide[reach : reach + ROWS] = grad[...].astype(F32)
    wide[reach + ROWS :] = after[...].astype(F32)
    for chunk in range(ROWS // CHUNK):
        row0 = chunk * CHUNK
        running = base[row0 : row0 + CHUNK].astype(F32)
        for index in range(TAPS):
            begin = row0 + (TAPS - 1 - index) * gap
            tap = conv[layer, index : index + 1].astype(F32)
            running = running + tap * wide[begin : begin + CHUNK]
        out[row0 : row0 + CHUNK] = running.astype(BF16)


def spread(base, grad, before, after, conv, layer, gap):
    def kernel(*refs):
        spread_kernel(*refs, layer=layer, gap=gap)

    scratch = [pltpu.VMEM((ROWS + gap * (TAPS - 1), LANES), F32)]
    out = shape((ROWS, LANES), BF16)
    return call(kernel, out, scratch, None, base, grad, before, after, conv)


def seq_shift(cells, step):
    count = lax.axis_size(SEQ)
    if step > 0:
        return lax.ppermute(cells, SEQ, [(i, i + 1) for i in range(count - 1)])
    return lax.ppermute(cells, SEQ, [(i + 1, i) for i in range(count - 1)])


def ring_copies(slab):
    count = lax.axis_size("zh")
    moved = {0: slab}
    for step in (2, 1, 3):
        moved[step] = lax.ppermute(slab, "zh", [(i, (i + step) % count) for i in range(count)])
    return [moved[step] for step in STEPS]


def core_swap(cells):
    return lax.ppermute(cells, "core", [(0, 1), (1, 0)])


def on_device(
    base_ids, span_start, span_length, embedding, conv_kernel, mix_weight, saved_input, cotangent
):
    total_rows = ROWS * lax.axis_size(SEQ)
    place = jnp.stack(
        [
            lax.axis_index(SEQ),
            jnp.int32(total_rows),
            lax.axis_index("zh"),
            lax.axis_index("core"),
            lax.axis_index("zl"),
        ]
    ).astype(jnp.int32)
    smem = pl.BlockSpec(memory_space=pltpu.SMEM)
    vmem = pl.BlockSpec(memory_space=pltpu.VMEM)
    ids = base_ids.reshape(ROWS // 128, 128)
    slab = shape((ROWS, LANES), BF16)
    slab_wide = shape((ROWS, LANES), F32)
    turned = shape((LANES, ROWS), BF16)

    message = shape((MESSAGE, LANES), BF16)
    to_next, to_prev = call_staged(
        pack_kernel, (message, message), [], None, saved_input, ids
    )
    before = seq_shift(to_next, 1)
    after = seq_shift(to_prev, -1)
    mine = ring_copies(cotangent)

    slope_up, act_up, slope_low, act_low, masked, hot = call_staged(
        prep_kernel,
        (slab_wide, turned, slab_wide, turned, slab, shape((128, ROWS), BF16)),
        [
            pltpu.VMEM((ROWS + 2 * CHUNK, 128), F32),
            pltpu.VMEM((ROWS + 2 * LOW_REACH, 128), F32),
            pltpu.VMEM((ROWS + 2 * HIGH_REACH, LANES), F32),
            pltpu.VMEM((ROWS + 2 * LOW_REACH, LANES), F32),
            pltpu.VMEM((128, LANES), F32),
            pltpu.VMEM((ROWS, LANES), BF16),
        ],
        place, before, after, saved_input, cotangent, ids,
        span_start.reshape(-1, 128), span_length.reshape(-1, 128), embedding, conv_kernel,
    )
    own = core_swap(mine[0])
    slope_up, own, mine[1], mine[2], mine[3] = lax.optimization_barrier(
        (slope_up, own, mine[1], mine[2], mine[3])
    )
    pairs = own, core_swap(jnp.stack(mine[1:]))

    weight_specs = [
        pl.BlockSpec((1, LANES, 8 * LANES), lambda step: (0, 0, 0)),
        pl.BlockSpec((1, LANES, 8 * LANES), lambda step: (1, 0, 0)),
    ]
    rim = shape((HIGH_REACH, LANES), BF16)
    grad_upper, head, tail = call(
        upper_kernel,
        (slab, rim, rim),
        [],
        [smem] + [vmem] * 6 + [weight_specs[1], vmem],
        place, *mine, *pairs, mix_weight, slope_up,
    )
    up_before = seq_shift(tail, 1)
    up_after = seq_shift(head, -1)
    up_mid = spread(masked, grad_upper, up_before, up_after, conv_kernel, 1, HIGH_GAP)
    mid = ring_copies(up_mid)
    mid_pairs = core_swap(jnp.stack(mid[:2])), core_swap(jnp.stack(mid[2:]))

    far_specs = (pl.BlockSpec(memory_space=pltpu.HBM), vmem)
    upper_outer, upper_taps = call(
        upper_outer_kernel,
        (pltpu.HBM((LANES, 8 * LANES), BF16), shape((16, LANES), F32)),
        [
            pltpu.VMEM((ROWS + 2 * HIGH_REACH, LANES), F32),
            pltpu.VMEM((LANES, 8 * LANES), BF16),
            pltpu.SemaphoreType.DMA((8,)),
        ],
        [vmem] * 11,
        act_up, *mine, *pairs, grad_upper, before, saved_input, after, out_specs=far_specs,
    )
    pieces = lax.all_to_all(upper_outer.reshape(8, 32, 8 * LANES), NEAR, 0, 0)
    upper_sum = call(upper_sum_kernel, shape((32, 8 * LANES), BF16), [], None, pieces)

    lower_outer, grad_lower = call(
        lower_kernel,
        (pltpu.HBM((LANES, 9 * LANES), BF16), slab),
        [
            pltpu.VMEM((32, LANES), F32),
            pltpu.VMEM((8, LANES), F32),
            pltpu.VMEM((LANES, 9 * LANES), BF16),
            pltpu.SemaphoreType.DMA((9,)),
        ],
        [smem] + [vmem] * 7 + [weight_specs[0]] + [vmem] * 6,
        place, act_low, *mid, *mid_pairs, mix_weight, slope_low, hot, up_mid, embedding,
        conv_kernel, upper_taps, out_specs=far_specs, cost=LOWER_COST,
    )
    pieces = lax.all_to_all(lower_outer.reshape(8, 32, 9 * LANES), NEAR, 0, 0)
    low_before = seq_shift(grad_lower[ROWS - LOW_REACH :], 1)
    low_after = seq_shift(grad_lower[:LOW_REACH], -1)
    input_grad = spread(up_mid, grad_lower, low_before, low_after, conv_kernel, 0, LOW_GAP)
    middle = call(
        middle_kernel, shape((8, 4, 22 * LANES), BF16), [], None, pieces, upper_sum
    )
    pieces = lax.all_to_all(middle, "y", 0, 0)

    def finish(*refs):
        final_kernel(*refs, scale=1.0 / math.sqrt(total_rows))

    weight_grad, kernel_grad, embed_grad = call(
        finish,
        (shape((2, 4, 8 * LANES), F32), shape((TAPS, 2, LANES), F32), shape((VOCAB, LANES), F32)),
        [],
        [smem, vmem],
        place, pieces,
    )
    return (input_grad, weight_grad, kernel_grad.transpose(1, 0, 2), embed_grad)


def solution(mesh):
    fine = Mesh(mesh.devices.reshape(8, 2, 4, 4, 2), SEQ + BLK)
    placed = (
        P(SEQ),
        P(),
        P(),
        P(None, BLK),
        P(None, None, BLK),
        P(None, BLK, None),
        P(SEQ, BLK),
        P(SEQ, BLK),
    )
    return jax.shard_map(
        on_device,
        mesh=fine,
        in_specs=placed,
        out_specs=(
            P(SEQ, BLK),
            P(None, BLK + SEQ, None),
            P(None, None, BLK),
            P(None, BLK),
        ),
        check_vma=False,
    )
```

```python
import math

import jax
import jax.numpy as jnp
from jax import lax
from jax.experimental import pallas as pl
from jax.experimental.pallas import tpu as pltpu
from jax.sharding import Mesh, PartitionSpec as P

BASE_DILATION = 4

SEQ = ("y", "zl", "x")
BLK = ("zh", "core")
NEAR = ("zl", "x")
STEPS = (0, 1, 3, 2)

mask_token = 4
gelu_scale = 0.7978845608028654
gelu_cubic = 0.044715
LANES = 256
BF16 = jnp.bfloat16
F32 = jnp.float32

ROWS = 512
TAPS = 9
VOCAB = 5
LOW_GAP, HIGH_GAP = BASE_DILATION, 2 * BASE_DILATION
LOW_REACH, HIGH_REACH = 4 * LOW_GAP, 4 * HIGH_GAP
EDGE = HIGH_REACH
MESSAGE = EDGE + 16
CHUNK = 64
LOWER_COST = 10000000000
PAIRED = (((1,), (1,)), ((), ()))


def gelu_pair(pre_act):
    square = pre_act * pre_act
    tangent = jnp.tanh(gelu_scale * (pre_act + gelu_cubic * square * pre_act))
    half = 0.5 * (1.0 + tangent)
    derivative = half + 0.5 * pre_act * (1.0 - tangent * tangent) * gelu_scale * (
        1.0 + 3.0 * gelu_cubic * square
    )
    return (pre_act * half, derivative)


def call(kernel, outs, scratch, in_specs, *operands, out_specs=None, cost=None):
    extra = {} if in_specs is None else {"in_specs": in_specs, "grid": (1,)}
    if cost is not None:
        extra["cost_estimate"] = pl.CostEstimate(
            flops=cost, transcendentals=0, bytes_accessed=0
        )
    if out_specs is not None:
        extra["out_specs"] = out_specs
    return pl.pallas_call(
        kernel,
        out_shape=outs,
        scratch_shapes=scratch,
        compiler_params=pltpu.CompilerParams(vmem_limit_bytes=16 << 20),
        **extra,
    )(*operands)


def call_staged(kernel, outs, scratch, place, *operands):
    count = len(operands)
    lead = 0 if place is None else 1

    def staged(*refs):
        head, sources, rest = refs[:lead], refs[lead : lead + count], refs[lead + count :]
        held, sems = rest[-count - 1 : -1], rest[-1]
        loads = [
            pltpu.make_async_copy(sources[index], held[index], sems.at[index])
            for index in range(count)
        ]
        for load in loads:
            load.start()
        for load in loads:
            load.wait()
        kernel(*head, *held, *rest[: -count - 1])

    smem = pl.BlockSpec(memory_space=pltpu.SMEM)
    hbm = pl.BlockSpec(memory_space=pltpu.HBM)
    operands = [pltpu.with_memory_space_constraint(cells, pltpu.HBM) for cells in operands]
    return pl.pallas_call(
        staged,
        out_shape=outs,
        in_specs=[smem] * lead + [hbm] * count,
        scratch_shapes=list(scratch)
        + [pltpu.VMEM(cells.shape, cells.dtype) for cells in operands]
        + [pltpu.SemaphoreType.DMA((count,))],
        compiler_params=pltpu.CompilerParams(vmem_limit_bytes=24 << 20),
    )(*(() if place is None else (place,)), *operands)


def shape(dims, kind):
    return jax.ShapeDtypeStruct(dims, kind)


def pack_kernel(saved, ids, next_out, prev_out):
    for out, begin, row in ((next_out, ROWS - EDGE, 3), (prev_out, 0, 0)):
        out[:EDGE] = saved[begin : begin + EDGE]
        line = jnp.broadcast_to(ids[row : row + 1].astype(F32), (MESSAGE - EDGE, 128))
        out[EDGE:] = jnp.concatenate([line, line], axis=1).astype(BF16)


def prep_kernel(
    place, before, after, saved, cot, ids, start, length, embedding, conv,
    slope_up, act_up, slope_low, act_low, masked, hot_out,
    cover, idw, wide, first, table, act_all,
):
    base = place[0] * ROWS - CHUNK
    total = place[1]

    def cover_chunk(index, carry):
        row0 = pl.multiple_of(index * CHUNK, CHUNK)
        here = lax.broadcasted_iota(jnp.int32, (CHUNK, 128), 0) + (base + row0)
        hit = jnp.zeros((CHUNK, 128), jnp.int32)
        for group in range(start.shape[0]):
            gap = here - start[group : group + 1]
            hit = jnp.where((gap >= 0) & (gap < length[group : group + 1]), 1, hit)
        seen = jnp.max(hit, axis=1, keepdims=True).astype(F32)
        cover[pl.ds(row0, CHUNK), :] = jnp.broadcast_to(seen, (CHUNK, 128))
        return carry

    lax.fori_loop(0, ROWS // CHUNK + 2, cover_chunk, 0)

    def column(row):
        return jnp.transpose(jnp.broadcast_to(row.astype(F32), (128, 128)))

    idw[:LOW_REACH] = column(before[EDGE : EDGE + 1, :128])[128 - LOW_REACH :]
    for piece in range(ROWS // 128):
        idw[LOW_REACH + 128 * piece : LOW_REACH + 128 * (piece + 1)] = column(ids[piece : piece + 1])
    idw[LOW_REACH + ROWS :] = column(after[EDGE : EDGE + 1, :128])[:LOW_REACH]
    spread = ROWS + 2 * LOW_REACH
    spot = lax.broadcasted_iota(jnp.int32, (spread, 128), 0) + (base + CHUNK - LOW_REACH)
    lane = lax.broadcasted_iota(jnp.int32, (1, 128), 1)
    tokens = jnp.where(
        cover[CHUNK - LOW_REACH : CHUNK - LOW_REACH + spread] > 0.0,
        float(mask_token),
        idw[...],
    )
    tokens = jnp.where((spot >= 0) & (spot < total), tokens, 7.0)
    idw[...] = tokens
    table[...] = jnp.zeros_like(table)
    table[:VOCAB] = embedding[...].astype(F32)
    hot = jnp.where(tokens == lane.astype(F32), 1.0, 0.0).astype(BF16)
    first[...] = jnp.dot(hot, table[...].astype(BF16), preferred_element_type=F32)

    channel = lax.broadcasted_iota(jnp.int32, (LANES, LANES), 1)
    target = lax.broadcasted_iota(jnp.int32, (LANES, LANES), 0)
    tail = ((channel >> 5) << 2) | (channel & 3)
    low_place = (((channel >> 2) & 7) << 5) | tail
    low_shuffle = jnp.where(low_place == target, 1.0, 0.0).astype(BF16)

    taps_low = [conv[0, index : index + 1].astype(F32) for index in range(TAPS)]
    for chunk in range(ROWS // CHUNK):
        row0 = chunk * CHUNK
        pre = None
        for index in range(TAPS):
            begin = row0 + index * LOW_GAP
            term = taps_low[index] * first[begin : begin + CHUNK]
            pre = term if pre is None else pre + term
        act, slope = gelu_pair(pre)
        slope_low[row0 : row0 + CHUNK] = slope
        act_all[row0 : row0 + CHUNK] = act.astype(BF16)
    act_low[...] = lax.dot_general(
        low_shuffle, act_all[:ROWS], PAIRED, preferred_element_type=F32
    ).astype(BF16)

    picked = idw[:ROWS]
    for index in range(1, TAPS):
        picked = jnp.where((lane >> 3) == index, idw[index * LOW_GAP : index * LOW_GAP + ROWS], picked)
    kind = lane & 7
    live = (kind < VOCAB) & (lane < 8 * TAPS)
    hot = jnp.where((picked == kind.astype(F32)) & live, 1.0, 0.0)
    hot_out[...] = jnp.transpose(hot).astype(BF16)

    wide[:HIGH_REACH] = before[:HIGH_REACH].astype(F32)
    wide[HIGH_REACH : HIGH_REACH + ROWS] = saved[...].astype(F32)
    wide[HIGH_REACH + ROWS :] = after[:HIGH_REACH].astype(F32)
    taps_up = [conv[1, index : index + 1].astype(F32) for index in range(TAPS)]
    for chunk in range(ROWS // CHUNK):
        row0 = chunk * CHUNK
        pre = None
        for index in range(TAPS):
            begin = row0 + index * HIGH_GAP
            term = taps_up[index] * wide[begin : begin + CHUNK]
            pre = term if pre is None else pre + term
        act, slope = gelu_pair(pre)
        seen = cover[CHUNK + row0 : 2 * CHUNK + row0] > 0.0
        seen = jnp.concatenate([seen, seen], axis=1)
        slope_up[row0 : row0 + CHUNK] = jnp.where(seen, slope, 0.0)
        act_all[row0 : row0 + CHUNK] = jnp.where(seen, act, 0.0).astype(BF16)
        masked[row0 : row0 + CHUNK] = jnp.where(
            seen, cot[row0 : row0 + CHUNK].astype(F32), 0.0
        ).astype(BF16)
    act_up[...] = lax.dot_general(
        low_shuffle, act_all[:ROWS], PAIRED, preferred_element_type=F32
    ).astype(BF16)


def chip_block(place, step):
    return (place[2] - step) & 3


def weight_columns(weights, place, step, core):
    block = chip_block(place, step) * 2 + core
    return weights[0, :, pl.ds(pl.multiple_of(block * LANES, LANES), LANES)]


def product_over_blocks(place, mine, pairs, weights):
    total = None
    for index, step in enumerate(STEPS):
        term = lax.dot_general(
            mine[index][...], weight_columns(weights, place, step, place[3]), PAIRED,
            preferred_element_type=F32,
        )
        total = term if total is None else total + term
    for index, step in enumerate(STEPS):
        total = total + lax.dot_general(
            pairs[index // 2][index % 2], weight_columns(weights, place, step, 1 - place[3]),
            PAIRED, preferred_element_type=F32,
        )
    return total


def upper_kernel(place, m0, m1, m2, m3, p0, p1, weights, slope, grad_out, head_out, tail_out):
    grad = product_over_blocks(place, (m0, m1, m2, m3), (p0, p1), weights) * slope[...]
    grad = grad.astype(BF16)
    grad_out[...] = grad
    head_out[...] = grad[:HIGH_REACH]
    tail_out[...] = grad[ROWS - HIGH_REACH :]


def outer_product(act, mine, pairs, out, stage, sems):
    copies = []
    for index in range(2 * len(STEPS)):
        half = index % len(STEPS)
        piece = mine[half][...] if index < len(STEPS) else pairs[half // 2][half % 2]
        lanes = slice(index * LANES, (index + 1) * LANES)
        stage[:, lanes] = jnp.dot(act[...], piece, preferred_element_type=F32).astype(BF16)
        copies.append(
            pltpu.make_async_copy(stage.at[:, lanes], out.at[:, lanes], sems.at[index])
        )
        copies[-1].start()
    return copies


def upper_outer_kernel(
    act, m0, m1, m2, m3, p0, p1, grad, before, saved, after, out, tap_out, wide, stage, sems
):
    copies = outer_product(act, (m0, m1, m2, m3), (p0, p1), out, stage, sems)
    wide[:HIGH_REACH] = before[:HIGH_REACH].astype(F32)
    wide[HIGH_REACH : HIGH_REACH + ROWS] = saved[...].astype(F32)
    wide[HIGH_REACH + ROWS :] = after[:HIGH_REACH].astype(F32)
    sums = [jnp.zeros((8, LANES), F32) for index in range(TAPS)]
    for chunk in range(ROWS // CHUNK):
        row0 = chunk * CHUNK
        grad_wide = grad[row0 : row0 + CHUNK].astype(F32)
        for index in range(TAPS):
            begin = row0 + index * HIGH_GAP
            term = grad_wide * wide[begin : begin + CHUNK]
            sums[index] = sums[index] + jnp.sum(term.reshape(CHUNK // 8, 8, LANES), axis=0)
    tap_out[...] = jnp.zeros_like(tap_out)
    for index in range(TAPS):
        tap_out[index : index + 1] = jnp.sum(sums[index], axis=0, keepdims=True)
    for copy in copies:
        copy.wait()


def lower_kernel(
    place, act, m0, m1, m2, m3, p0, p1, weights, slope, hot, up_row, embedding, conv, upper_taps,
    out, grad_out, small, table, stage, sems,
):
    mine, pairs = (m0, m1, m2, m3), (p0, p1)
    grad = (product_over_blocks(place, mine, pairs, weights) * slope[...]).astype(BF16)
    grad_out[...] = grad
    copies = outer_product(act, mine, pairs, out, stage, sems)
    picked = jnp.dot(hot[...], grad, preferred_element_type=F32)
    embed = jnp.dot(hot[32:48], up_row[...], preferred_element_type=F32)[:8]
    table[...] = jnp.zeros_like(table)
    table[:VOCAB] = embedding[...].astype(F32)
    small[...] = jnp.zeros_like(small)
    for index in range(TAPS):
        piece = picked[index * 8 : index * 8 + 8]
        small[index : index + 1] = jnp.sum(piece * table[...], axis=0, keepdims=True)
        embed = embed + piece * conv[0, index : index + 1].astype(F32)
    small[TAPS : TAPS + VOCAB] = embed[:VOCAB]
    small[TAPS + VOCAB : 2 * TAPS + VOCAB] = upper_taps[:TAPS]
    packed = small[...].astype(BF16)
    for index in range(LANES // 32):
        stage[index * 32 : (index + 1) * 32, 8 * LANES :] = packed
    last = pltpu.make_async_copy(
        stage.at[:, 8 * LANES :], out.at[:, 8 * LANES :], sems.at[8]
    )
    last.start()
    for copy in copies + [last]:
        copy.wait()


def add_up(pieces):
    running = pieces[0].astype(F32)
    for index in range(1, pieces.shape[0]):
        running = running + pieces[index].astype(F32)
    return running


def upper_sum_kernel(pieces, out):
    out[...] = add_up(pieces).astype(BF16)


def middle_kernel(pieces, upper, out):
    running = pieces[0].astype(F32)
    for index in range(1, pieces.shape[0]):
        running = running + pieces[index].astype(F32)
    width = 8 * LANES
    upper = upper[...]
    small = running[:, width:].astype(BF16)
    lower = running[:, :width].astype(BF16)
    for far in range(8):
        out[far, :, :width] = lower[4 * far : 4 * far + 4]
        out[far, :, width : 2 * width] = upper[4 * far : 4 * far + 4]
        for group in range(6):
            begin = 2 * width + group * LANES
            out[far, :, begin : begin + LANES] = small[4 * group : 4 * group + 4]


def final_kernel(place, pieces, weight_out, kernel_out, embed_out, *, scale):
    running = pieces[0].astype(F32)
    for index in range(1, pieces.shape[0]):
        running = running + pieces[index].astype(F32)
    running = running * scale
    width = 8 * LANES
    for index in range(8):
        step = STEPS[index % 4]
        core = place[3] if index < 4 else 1 - place[3]
        spot = pl.multiple_of((chip_block(place, step) * 2 + core) * LANES, LANES)
        for layer in range(2):
            begin = layer * width + index * LANES
            weight_out[layer, :, pl.ds(spot, LANES)] = running[:, begin : begin + LANES]

    def small_row(row):
        begin = 2 * width + (row // 4) * LANES
        return running[row % 4 : row % 4 + 1, begin : begin + LANES]

    for index in range(TAPS):
        kernel_out[index, 0:1] = small_row(index)
        kernel_out[index, 1:2] = small_row(TAPS + VOCAB + index)
    for index in range(VOCAB):
        embed_out[index : index + 1] = small_row(TAPS + index)


def spread_kernel(base, grad, before, after, conv, out, wide, *, layer, gap):
    reach = gap * (TAPS // 2)
    wide[:reach] = before[...].astype(F32)
    wide[reach : reach + ROWS] = grad[...].astype(F32)
    wide[reach + ROWS :] = after[...].astype(F32)
    for chunk in range(ROWS // CHUNK):
        row0 = chunk * CHUNK
        running = base[row0 : row0 + CHUNK].astype(F32)
        for index in range(TAPS):
            begin = row0 + (TAPS - 1 - index) * gap
            tap = conv[layer, index : index + 1].astype(F32)
            running = running + tap * wide[begin : begin + CHUNK]
        out[row0 : row0 + CHUNK] = running.astype(BF16)


def spread(base, grad, before, after, conv, layer, gap):
    def kernel(*refs):
        spread_kernel(*refs, layer=layer, gap=gap)

    scratch = [pltpu.VMEM((ROWS + gap * (TAPS - 1), LANES), F32)]
    out = shape((ROWS, LANES), BF16)
    return call(kernel, out, scratch, None, base, grad, before, after, conv)


def seq_shift(cells, step):
    count = lax.axis_size(SEQ)
    if step > 0:
        return lax.ppermute(cells, SEQ, [(i, i + 1) for i in range(count - 1)])
    return lax.ppermute(cells, SEQ, [(i + 1, i) for i in range(count - 1)])


def ring_copies(slab):
    count = lax.axis_size("zh")
    moved = {0: slab}
    for step in (2, 1, 3):
        moved[step] = lax.ppermute(slab, "zh", [(i, (i + step) % count) for i in range(count)])
    return [moved[step] for step in STEPS]


def core_swap(cells):
    return lax.ppermute(cells, "core", [(0, 1), (1, 0)])


def swapped_pairs(mine):
    return core_swap(jnp.stack(mine[:2])), core_swap(jnp.stack(mine[2:]))


def on_device(
    base_ids, span_start, span_length, embedding, conv_kernel, mix_weight, saved_input, cotangent
):
    total_rows = ROWS * lax.axis_size(SEQ)
    place = jnp.stack(
        [
            lax.axis_index(SEQ),
            jnp.int32(total_rows),
            lax.axis_index("zh"),
            lax.axis_index("core"),
            lax.axis_index("zl"),
        ]
    ).astype(jnp.int32)
    smem = pl.BlockSpec(memory_space=pltpu.SMEM)
    vmem = pl.BlockSpec(memory_space=pltpu.VMEM)
    ids = base_ids.reshape(ROWS // 128, 128)
    slab = shape((ROWS, LANES), BF16)
    slab_wide = shape((ROWS, LANES), F32)
    turned = shape((LANES, ROWS), BF16)

    message = shape((MESSAGE, LANES), BF16)
    to_next, to_prev = call_staged(
        pack_kernel, (message, message), [], None, saved_input, ids
    )
    before = seq_shift(to_next, 1)
    after = seq_shift(to_prev, -1)
    mine = ring_copies(cotangent)

    slope_up, act_up, slope_low, act_low, masked, hot = call_staged(
        prep_kernel,
        (slab_wide, turned, slab_wide, turned, slab, shape((128, ROWS), BF16)),
        [
            pltpu.VMEM((ROWS + 2 * CHUNK, 128), F32),
            pltpu.VMEM((ROWS + 2 * LOW_REACH, 128), F32),
            pltpu.VMEM((ROWS + 2 * HIGH_REACH, LANES), F32),
            pltpu.VMEM((ROWS + 2 * LOW_REACH, LANES), F32),
            pltpu.VMEM((128, LANES), F32),
            pltpu.VMEM((ROWS, LANES), BF16),
        ],
        place, before, after, saved_input, cotangent, ids,
        span_start.reshape(-1, 128), span_length.reshape(-1, 128), embedding, conv_kernel,
    )
    slope_up, mine[1], mine[2], mine[3] = lax.optimization_barrier(
        (slope_up, mine[1], mine[2], mine[3])
    )
    pairs = swapped_pairs(mine)

    weight_specs = [
        pl.BlockSpec((1, LANES, 8 * LANES), lambda step: (0, 0, 0)),
        pl.BlockSpec((1, LANES, 8 * LANES), lambda step: (1, 0, 0)),
    ]
    rim = shape((HIGH_REACH, LANES), BF16)
    grad_upper, head, tail = call(
        upper_kernel,
        (slab, rim, rim),
        [],
        [smem] + [vmem] * 6 + [weight_specs[1], vmem],
        place, *mine, *pairs, mix_weight, slope_up,
    )
    up_before = seq_shift(tail, 1)
    up_after = seq_shift(head, -1)
    up_mid = spread(masked, grad_upper, up_before, up_after, conv_kernel, 1, HIGH_GAP)
    mid = ring_copies(up_mid)
    mid_pairs = swapped_pairs(mid)

    far_specs = (pl.BlockSpec(memory_space=pltpu.HBM), vmem)
    upper_outer, upper_taps = call(
        upper_outer_kernel,
        (pltpu.HBM((LANES, 8 * LANES), BF16), shape((16, LANES), F32)),
        [
            pltpu.VMEM((ROWS + 2 * HIGH_REACH, LANES), F32),
            pltpu.VMEM((LANES, 8 * LANES), BF16),
            pltpu.SemaphoreType.DMA((8,)),
        ],
        [vmem] * 11,
        act_up, *mine, *pairs, grad_upper, before, saved_input, after, out_specs=far_specs,
    )
    pieces = lax.all_to_all(upper_outer.reshape(8, 32, 8 * LANES), NEAR, 0, 0)
    upper_sum = call(upper_sum_kernel, shape((32, 8 * LANES), BF16), [], None, pieces)

    lower_outer, grad_lower = call(
        lower_kernel,
        (pltpu.HBM((LANES, 9 * LANES), BF16), slab),
        [
            pltpu.VMEM((32, LANES), F32),
            pltpu.VMEM((8, LANES), F32),
            pltpu.VMEM((LANES, 9 * LANES), BF16),
            pltpu.SemaphoreType.DMA((9,)),
        ],
        [smem] + [vmem] * 7 + [weight_specs[0]] + [vmem] * 6,
        place, act_low, *mid, *mid_pairs, mix_weight, slope_low, hot, up_mid, embedding,
        conv_kernel, upper_taps, out_specs=far_specs, cost=LOWER_COST,
    )
    pieces = lax.all_to_all(lower_outer.reshape(8, 32, 9 * LANES), NEAR, 0, 0)
    low_before = seq_shift(grad_lower[ROWS - LOW_REACH :], 1)
    low_after = seq_shift(grad_lower[:LOW_REACH], -1)
    input_grad = spread(up_mid, grad_lower, low_before, low_after, conv_kernel, 0, LOW_GAP)
    pieces, input_grad = lax.optimization_barrier((pieces, input_grad))
    middle = call(
        middle_kernel, shape((8, 4, 22 * LANES), BF16), [], None, pieces, upper_sum
    )
    pieces = lax.all_to_all(middle, "y", 0, 0)

    def finish(*refs):
        final_kernel(*refs, scale=1.0 / math.sqrt(total_rows))

    weight_grad, kernel_grad, embed_grad = call(
        finish,
        (shape((2, 4, 8 * LANES), F32), shape((TAPS, 2, LANES), F32), shape((VOCAB, LANES), F32)),
        [],
        [smem, vmem],
        place, pieces,
    )
    return (input_grad, weight_grad, kernel_grad.transpose(1, 0, 2), embed_grad)


def solution(mesh):
    fine = Mesh(mesh.devices.reshape(8, 2, 4, 4, 2), SEQ + BLK)
    placed = (
        P(SEQ),
        P(),
        P(),
        P(None, BLK),
        P(None, None, BLK),
        P(None, BLK, None),
        P(SEQ, BLK),
        P(SEQ, BLK),
    )
    return jax.shard_map(
        on_device,
        mesh=fine,
        in_specs=placed,
        out_specs=(
            P(SEQ, BLK),
            P(None, BLK + SEQ, None),
            P(None, None, BLK),
            P(None, BLK),
        ),
        check_vma=False,
    )
```

```python
import math

import jax
import jax.numpy as jnp
from jax import lax
from jax.experimental import pallas as pl
from jax.experimental.pallas import tpu as pltpu
from jax.sharding import Mesh, PartitionSpec as P

BASE_DILATION = 4

SEQ = ("y", "zl", "x")
BLK = ("zh", "core")
NEAR = ("zl", "x")
STEPS = (0, 1, 3, 2)

mask_token = 4
gelu_scale = 0.7978845608028654
gelu_cubic = 0.044715
LANES = 256
BF16 = jnp.bfloat16
F32 = jnp.float32

ROWS = 512
TAPS = 9
VOCAB = 5
LOW_GAP, HIGH_GAP = BASE_DILATION, 2 * BASE_DILATION
LOW_REACH, HIGH_REACH = 4 * LOW_GAP, 4 * HIGH_GAP
EDGE = HIGH_REACH
MESSAGE = EDGE + 16
CHUNK = 64
LOWER_COST = 10000000000
PAIRED = (((1,), (1,)), ((), ()))


def gelu_pair(pre_act):
    square = pre_act * pre_act
    tangent = jnp.tanh(gelu_scale * (pre_act + gelu_cubic * square * pre_act))
    half = 0.5 * (1.0 + tangent)
    derivative = half + 0.5 * pre_act * (1.0 - tangent * tangent) * gelu_scale * (
        1.0 + 3.0 * gelu_cubic * square
    )
    return (pre_act * half, derivative)


def call(kernel, outs, scratch, in_specs, *operands, out_specs=None, cost=None):
    extra = {} if in_specs is None else {"in_specs": in_specs, "grid": (1,)}
    if cost is not None:
        extra["cost_estimate"] = pl.CostEstimate(
            flops=cost, transcendentals=0, bytes_accessed=0
        )
    if out_specs is not None:
        extra["out_specs"] = out_specs
    return pl.pallas_call(
        kernel,
        out_shape=outs,
        scratch_shapes=scratch,
        compiler_params=pltpu.CompilerParams(vmem_limit_bytes=16 << 20),
        **extra,
    )(*operands)


def call_staged(kernel, outs, scratch, place, *operands):
    count = len(operands)
    lead = 0 if place is None else 1

    def staged(*refs):
        head, sources, rest = refs[:lead], refs[lead : lead + count], refs[lead + count :]
        held, sems = rest[-count - 1 : -1], rest[-1]
        loads = [
            pltpu.make_async_copy(sources[index], held[index], sems.at[index])
            for index in range(count)
        ]
        for load in loads:
            load.start()
        for load in loads:
            load.wait()
        kernel(*head, *held, *rest[: -count - 1])

    smem = pl.BlockSpec(memory_space=pltpu.SMEM)
    hbm = pl.BlockSpec(memory_space=pltpu.HBM)
    operands = [pltpu.with_memory_space_constraint(cells, pltpu.HBM) for cells in operands]
    return pl.pallas_call(
        staged,
        out_shape=outs,
        in_specs=[smem] * lead + [hbm] * count,
        scratch_shapes=list(scratch)
        + [pltpu.VMEM(cells.shape, cells.dtype) for cells in operands]
        + [pltpu.SemaphoreType.DMA((count,))],
        compiler_params=pltpu.CompilerParams(vmem_limit_bytes=24 << 20),
    )(*(() if place is None else (place,)), *operands)


def shape(dims, kind):
    return jax.ShapeDtypeStruct(dims, kind)


def pack_kernel(saved, ids, next_out, prev_out):
    for out, begin, row in ((next_out, ROWS - EDGE, 3), (prev_out, 0, 0)):
        out[:EDGE] = saved[begin : begin + EDGE]
        line = jnp.broadcast_to(ids[row : row + 1].astype(F32), (MESSAGE - EDGE, 128))
        out[EDGE:] = jnp.concatenate([line, line], axis=1).astype(BF16)


def prep_kernel(
    place, before, after, saved, cot, ids, start, length, embedding, conv,
    slope_up, act_up, slope_low, act_low, masked, hot_out,
    cover, idw, wide, first, table, act_all,
):
    base = place[0] * ROWS - CHUNK
    total = place[1]

    def cover_chunk(index, carry):
        row0 = pl.multiple_of(index * CHUNK, CHUNK)
        here = lax.broadcasted_iota(jnp.int32, (CHUNK, 128), 0) + (base + row0)
        hit = jnp.zeros((CHUNK, 128), jnp.int32)
        for group in range(start.shape[0]):
            gap = here - start[group : group + 1]
            hit = jnp.where((gap >= 0) & (gap < length[group : group + 1]), 1, hit)
        seen = jnp.max(hit, axis=1, keepdims=True).astype(F32)
        cover[pl.ds(row0, CHUNK), :] = jnp.broadcast_to(seen, (CHUNK, 128))
        return carry

    lax.fori_loop(0, ROWS // CHUNK + 2, cover_chunk, 0)

    def column(row):
        return jnp.transpose(jnp.broadcast_to(row.astype(F32), (128, 128)))

    idw[:LOW_REACH] = column(before[EDGE : EDGE + 1, :128])[128 - LOW_REACH :]
    for piece in range(ROWS // 128):
        idw[LOW_REACH + 128 * piece : LOW_REACH + 128 * (piece + 1)] = column(ids[piece : piece + 1])
    idw[LOW_REACH + ROWS :] = column(after[EDGE : EDGE + 1, :128])[:LOW_REACH]
    spread = ROWS + 2 * LOW_REACH
    spot = lax.broadcasted_iota(jnp.int32, (spread, 128), 0) + (base + CHUNK - LOW_REACH)
    lane = lax.broadcasted_iota(jnp.int32, (1, 128), 1)
    tokens = jnp.where(
        cover[CHUNK - LOW_REACH : CHUNK - LOW_REACH + spread] > 0.0,
        float(mask_token),
        idw[...],
    )
    tokens = jnp.where((spot >= 0) & (spot < total), tokens, 7.0)
    idw[...] = tokens
    table[...] = jnp.zeros_like(table)
    table[:VOCAB] = embedding[...].astype(F32)
    hot = jnp.where(tokens == lane.astype(F32), 1.0, 0.0).astype(BF16)
    first[...] = jnp.dot(hot, table[...].astype(BF16), preferred_element_type=F32)

    channel = lax.broadcasted_iota(jnp.int32, (LANES, LANES), 1)
    target = lax.broadcasted_iota(jnp.int32, (LANES, LANES), 0)
    tail = ((channel >> 5) << 2) | (channel & 3)
    low_place = (((channel >> 2) & 7) << 5) | tail
    low_shuffle = jnp.where(low_place == target, 1.0, 0.0).astype(BF16)

    taps_low = [conv[0, index : index + 1].astype(F32) for index in range(TAPS)]
    for chunk in range(ROWS // CHUNK):
        row0 = chunk * CHUNK
        pre = None
        for index in range(TAPS):
            begin = row0 + index * LOW_GAP
            term = taps_low[index] * first[begin : begin + CHUNK]
            pre = term if pre is None else pre + term
        act, slope = gelu_pair(pre)
        slope_low[row0 : row0 + CHUNK] = slope
        act_all[row0 : row0 + CHUNK] = act.astype(BF16)
    act_low[...] = lax.dot_general(
        low_shuffle, act_all[:ROWS], PAIRED, preferred_element_type=F32
    ).astype(BF16)

    picked = idw[:ROWS]
    for index in range(1, TAPS):
        picked = jnp.where((lane >> 3) == index, idw[index * LOW_GAP : index * LOW_GAP + ROWS], picked)
    kind = lane & 7
    live = (kind < VOCAB) & (lane < 8 * TAPS)
    hot = jnp.where((picked == kind.astype(F32)) & live, 1.0, 0.0)
    hot_out[...] = jnp.transpose(hot).astype(BF16)

    wide[:HIGH_REACH] = before[:HIGH_REACH].astype(F32)
    wide[HIGH_REACH : HIGH_REACH + ROWS] = saved[...].astype(F32)
    wide[HIGH_REACH + ROWS :] = after[:HIGH_REACH].astype(F32)
    taps_up = [conv[1, index : index + 1].astype(F32) for index in range(TAPS)]
    for chunk in range(ROWS // CHUNK):
        row0 = chunk * CHUNK
        pre = None
        for index in range(TAPS):
            begin = row0 + index * HIGH_GAP
            term = taps_up[index] * wide[begin : begin + CHUNK]
            pre = term if pre is None else pre + term
        act, slope = gelu_pair(pre)
        seen = cover[CHUNK + row0 : 2 * CHUNK + row0] > 0.0
        seen = jnp.concatenate([seen, seen], axis=1)
        slope_up[row0 : row0 + CHUNK] = jnp.where(seen, slope, 0.0)
        act_all[row0 : row0 + CHUNK] = jnp.where(seen, act, 0.0).astype(BF16)
        masked[row0 : row0 + CHUNK] = jnp.where(
            seen, cot[row0 : row0 + CHUNK].astype(F32), 0.0
        ).astype(BF16)
    act_up[...] = lax.dot_general(
        low_shuffle, act_all[:ROWS], PAIRED, preferred_element_type=F32
    ).astype(BF16)


def chip_block(place, step):
    return (place[2] - step) & 3


def weight_columns(weights, place, step, core):
    block = chip_block(place, step) * 2 + core
    return weights[0, :, pl.ds(pl.multiple_of(block * LANES, LANES), LANES)]


def product_over_blocks(place, mine, pairs, weights):
    total = None
    for index, step in enumerate(STEPS):
        term = lax.dot_general(
            mine[index][...], weight_columns(weights, place, step, place[3]), PAIRED,
            preferred_element_type=F32,
        )
        total = term if total is None else total + term
    for index, step in enumerate(STEPS):
        total = total + lax.dot_general(
            pairs[index // 2][index % 2], weight_columns(weights, place, step, 1 - place[3]),
            PAIRED, preferred_element_type=F32,
        )
    return total


def upper_kernel(place, m0, m1, m2, m3, p0, p1, weights, slope, grad_out, head_out, tail_out):
    grad = product_over_blocks(place, (m0, m1, m2, m3), (p0, p1), weights) * slope[...]
    grad = grad.astype(BF16)
    grad_out[...] = grad
    head_out[...] = grad[:HIGH_REACH]
    tail_out[...] = grad[ROWS - HIGH_REACH :]


def outer_product(act, mine, pairs, out, stage, sems):
    copies = []
    for index in range(2 * len(STEPS)):
        half = index % len(STEPS)
        piece = mine[half][...] if index < len(STEPS) else pairs[half // 2][half % 2]
        lanes = slice(index * LANES, (index + 1) * LANES)
        stage[:, lanes] = jnp.dot(act[...], piece, preferred_element_type=F32).astype(BF16)
        copies.append(
            pltpu.make_async_copy(stage.at[:, lanes], out.at[:, lanes], sems.at[index])
        )
        copies[-1].start()
    return copies


def upper_outer_kernel(
    act, m0, m1, m2, m3, p0, p1, grad, before, saved, after, out, tap_out, wide, stage, sems
):
    copies = outer_product(act, (m0, m1, m2, m3), (p0, p1), out, stage, sems)
    wide[:HIGH_REACH] = before[:HIGH_REACH].astype(F32)
    wide[HIGH_REACH : HIGH_REACH + ROWS] = saved[...].astype(F32)
    wide[HIGH_REACH + ROWS :] = after[:HIGH_REACH].astype(F32)
    sums = [jnp.zeros((8, LANES), F32) for index in range(TAPS)]
    for chunk in range(ROWS // CHUNK):
        row0 = chunk * CHUNK
        grad_wide = grad[row0 : row0 + CHUNK].astype(F32)
        for index in range(TAPS):
            begin = row0 + index * HIGH_GAP
            term = grad_wide * wide[begin : begin + CHUNK]
            sums[index] = sums[index] + jnp.sum(term.reshape(CHUNK // 8, 8, LANES), axis=0)
    tap_out[...] = jnp.zeros_like(tap_out)
    for index in range(TAPS):
        tap_out[index : index + 1] = jnp.sum(sums[index], axis=0, keepdims=True)
    for copy in copies:
        copy.wait()


def lower_kernel(
    place, act, m0, m1, m2, m3, p0, p1, weights, slope, hot, up_row, embedding, conv, upper_taps,
    out, grad_out, small, table, stage, sems,
):
    mine, pairs = (m0, m1, m2, m3), (p0, p1)
    grad = (product_over_blocks(place, mine, pairs, weights) * slope[...]).astype(BF16)
    grad_out[...] = grad
    copies = outer_product(act, mine, pairs, out, stage, sems)
    picked = jnp.dot(hot[...], grad, preferred_element_type=F32)
    embed = jnp.dot(hot[32:48], up_row[...], preferred_element_type=F32)[:8]
    table[...] = jnp.zeros_like(table)
    table[:VOCAB] = embedding[...].astype(F32)
    small[...] = jnp.zeros_like(small)
    for index in range(TAPS):
        piece = picked[index * 8 : index * 8 + 8]
        small[index : index + 1] = jnp.sum(piece * table[...], axis=0, keepdims=True)
        embed = embed + piece * conv[0, index : index + 1].astype(F32)
    small[TAPS : TAPS + VOCAB] = embed[:VOCAB]
    small[TAPS + VOCAB : 2 * TAPS + VOCAB] = upper_taps[:TAPS]
    packed = small[...].astype(BF16)
    for index in range(LANES // 32):
        stage[index * 32 : (index + 1) * 32, 8 * LANES :] = packed
    last = pltpu.make_async_copy(
        stage.at[:, 8 * LANES :], out.at[:, 8 * LANES :], sems.at[8]
    )
    last.start()
    for copy in copies + [last]:
        copy.wait()


def add_up(pieces):
    running = pieces[0].astype(F32)
    for index in range(1, pieces.shape[0]):
        running = running + pieces[index].astype(F32)
    return running


def upper_sum_kernel(pieces, out):
    out[...] = add_up(pieces).astype(BF16)


def middle_kernel(pieces, upper, out):
    running = pieces[0].astype(F32)
    for index in range(1, pieces.shape[0]):
        running = running + pieces[index].astype(F32)
    width = 8 * LANES
    upper = upper[...]
    small = running[:, width:].astype(BF16)
    lower = running[:, :width].astype(BF16)
    for far in range(8):
        out[far, :, :width] = lower[4 * far : 4 * far + 4]
        out[far, :, width : 2 * width] = upper[4 * far : 4 * far + 4]
        for group in range(6):
            begin = 2 * width + group * LANES
            out[far, :, begin : begin + LANES] = small[4 * group : 4 * group + 4]


def final_kernel(place, pieces, weight_out, kernel_out, embed_out, *, scale):
    running = pieces[0].astype(F32)
    for index in range(1, pieces.shape[0]):
        running = running + pieces[index].astype(F32)
    running = running * scale
    width = 8 * LANES
    for index in range(8):
        step = STEPS[index % 4]
        core = place[3] if index < 4 else 1 - place[3]
        spot = pl.multiple_of((chip_block(place, step) * 2 + core) * LANES, LANES)
        for layer in range(2):
            begin = layer * width + index * LANES
            weight_out[layer, :, pl.ds(spot, LANES)] = running[:, begin : begin + LANES]

    def small_row(row):
        begin = 2 * width + (row // 4) * LANES
        return running[row % 4 : row % 4 + 1, begin : begin + LANES]

    for index in range(TAPS):
        kernel_out[index, 0:1] = small_row(index)
        kernel_out[index, 1:2] = small_row(TAPS + VOCAB + index)
    for index in range(VOCAB):
        embed_out[index : index + 1] = small_row(TAPS + index)


def spread_kernel(base, grad, before, after, conv, out, wide, *, layer, gap):
    reach = gap * (TAPS // 2)
    wide[:reach] = before[...].astype(F32)
    wide[reach : reach + ROWS] = grad[...].astype(F32)
    wide[reach + ROWS :] = after[...].astype(F32)
    for chunk in range(ROWS // CHUNK):
        row0 = chunk * CHUNK
        running = base[row0 : row0 + CHUNK].astype(F32)
        for index in range(TAPS):
            begin = row0 + (TAPS - 1 - index) * gap
            tap = conv[layer, index : index + 1].astype(F32)
            running = running + tap * wide[begin : begin + CHUNK]
        out[row0 : row0 + CHUNK] = running.astype(BF16)


def spread(base, grad, before, after, conv, layer, gap):
    def kernel(*refs):
        spread_kernel(*refs, layer=layer, gap=gap)

    scratch = [pltpu.VMEM((ROWS + gap * (TAPS - 1), LANES), F32)]
    out = shape((ROWS, LANES), BF16)
    return call(kernel, out, scratch, None, base, grad, before, after, conv)


def seq_shift(cells, step):
    count = lax.axis_size(SEQ)
    if step > 0:
        return lax.ppermute(cells, SEQ, [(i, i + 1) for i in range(count - 1)])
    return lax.ppermute(cells, SEQ, [(i + 1, i) for i in range(count - 1)])


def ring_copies(slab):
    count = lax.axis_size("zh")
    moved = {0: slab}
    for step in (2, 1, 3):
        moved[step] = lax.ppermute(slab, "zh", [(i, (i + step) % count) for i in range(count)])
    return [moved[step] for step in STEPS]


def core_swap(cells):
    return lax.ppermute(cells, "core", [(0, 1), (1, 0)])


def swapped_pairs(mine):
    return core_swap(jnp.stack(mine[:2])), core_swap(jnp.stack(mine[2:]))


def on_device(
    base_ids, span_start, span_length, embedding, conv_kernel, mix_weight, saved_input, cotangent
):
    total_rows = ROWS * lax.axis_size(SEQ)
    place = jnp.stack(
        [
            lax.axis_index(SEQ),
            jnp.int32(total_rows),
            lax.axis_index("zh"),
            lax.axis_index("core"),
            lax.axis_index("zl"),
        ]
    ).astype(jnp.int32)
    smem = pl.BlockSpec(memory_space=pltpu.SMEM)
    vmem = pl.BlockSpec(memory_space=pltpu.VMEM)
    ids = base_ids.reshape(ROWS // 128, 128)
    slab = shape((ROWS, LANES), BF16)
    slab_wide = shape((ROWS, LANES), F32)
    turned = shape((LANES, ROWS), BF16)

    message = shape((MESSAGE, LANES), BF16)
    to_next, to_prev = call_staged(
        pack_kernel, (message, message), [], None, saved_input, ids
    )
    before = seq_shift(to_next, 1)
    after = seq_shift(to_prev, -1)
    mine = ring_copies(cotangent)

    slope_up, act_up, slope_low, act_low, masked, hot = call_staged(
        prep_kernel,
        (slab_wide, turned, slab_wide, turned, slab, shape((128, ROWS), BF16)),
        [
            pltpu.VMEM((ROWS + 2 * CHUNK, 128), F32),
            pltpu.VMEM((ROWS + 2 * LOW_REACH, 128), F32),
            pltpu.VMEM((ROWS + 2 * HIGH_REACH, LANES), F32),
            pltpu.VMEM((ROWS + 2 * LOW_REACH, LANES), F32),
            pltpu.VMEM((128, LANES), F32),
            pltpu.VMEM((ROWS, LANES), BF16),
        ],
        place, before, after, saved_input, cotangent, ids,
        span_start.reshape(-1, 128), span_length.reshape(-1, 128), embedding, conv_kernel,
    )
    slope_up, mine[1], mine[2], mine[3] = lax.optimization_barrier(
        (slope_up, mine[1], mine[2], mine[3])
    )
    pairs = swapped_pairs(mine)

    weight_specs = [
        pl.BlockSpec((1, LANES, 8 * LANES), lambda step: (0, 0, 0)),
        pl.BlockSpec((1, LANES, 8 * LANES), lambda step: (1, 0, 0)),
    ]
    rim = shape((HIGH_REACH, LANES), BF16)
    grad_upper, head, tail = call(
        upper_kernel,
        (slab, rim, rim),
        [],
        [smem] + [vmem] * 6 + [weight_specs[1], vmem],
        place, *mine, *pairs, mix_weight, slope_up,
    )
    up_before = seq_shift(tail, 1)
    up_after = seq_shift(head, -1)
    up_mid = spread(masked, grad_upper, up_before, up_after, conv_kernel, 1, HIGH_GAP)
    mid = ring_copies(up_mid)
    mid_pairs = swapped_pairs(mid)

    far_specs = (pl.BlockSpec(memory_space=pltpu.HBM), vmem)
    upper_outer, upper_taps = call(
        upper_outer_kernel,
        (pltpu.HBM((LANES, 8 * LANES), BF16), shape((16, LANES), F32)),
        [
            pltpu.VMEM((ROWS + 2 * HIGH_REACH, LANES), F32),
            pltpu.VMEM((LANES, 8 * LANES), BF16),
            pltpu.SemaphoreType.DMA((8,)),
        ],
        [vmem] * 11,
        act_up, *mine, *pairs, grad_upper, before, saved_input, after, out_specs=far_specs,
    )
    pieces = lax.all_to_all(upper_outer.reshape(8, 32, 8 * LANES), NEAR, 0, 0)
    upper_sum = call(upper_sum_kernel, shape((32, 8 * LANES), BF16), [], None, pieces)

    lower_outer, grad_lower = call(
        lower_kernel,
        (pltpu.HBM((LANES, 9 * LANES), BF16), slab),
        [
            pltpu.VMEM((32, LANES), F32),
            pltpu.VMEM((8, LANES), F32),
            pltpu.VMEM((LANES, 9 * LANES), BF16),
            pltpu.SemaphoreType.DMA((9,)),
        ],
        [smem] + [vmem] * 7 + [weight_specs[0]] + [vmem] * 6,
        place, act_low, *mid, *mid_pairs, mix_weight, slope_low, hot, up_mid, embedding,
        conv_kernel, upper_taps, out_specs=far_specs, cost=LOWER_COST,
    )
    pieces = lax.all_to_all(lower_outer.reshape(8, 32, 9 * LANES), NEAR, 0, 0)
    low_before = seq_shift(grad_lower[ROWS - LOW_REACH :], 1)
    low_after = seq_shift(grad_lower[:LOW_REACH], -1)
    pieces, low_before, low_after = lax.optimization_barrier((pieces, low_before, low_after))
    input_grad = spread(up_mid, grad_lower, low_before, low_after, conv_kernel, 0, LOW_GAP)
    middle = call(
        middle_kernel, shape((8, 4, 22 * LANES), BF16), [], None, pieces, upper_sum
    )
    pieces = lax.all_to_all(middle, "y", 0, 0)

    def finish(*refs):
        final_kernel(*refs, scale=1.0 / math.sqrt(total_rows))

    weight_grad, kernel_grad, embed_grad = call(
        finish,
        (shape((2, 4, 8 * LANES), F32), shape((TAPS, 2, LANES), F32), shape((VOCAB, LANES), F32)),
        [],
        [smem, vmem],
        place, pieces,
    )
    return (input_grad, weight_grad, kernel_grad.transpose(1, 0, 2), embed_grad)


def solution(mesh):
    fine = Mesh(mesh.devices.reshape(8, 2, 4, 4, 2), SEQ + BLK)
    placed = (
        P(SEQ),
        P(),
        P(),
        P(None, BLK),
        P(None, None, BLK),
        P(None, BLK, None),
        P(SEQ, BLK),
        P(SEQ, BLK),
    )
    return jax.shard_map(
        on_device,
        mesh=fine,
        in_specs=placed,
        out_specs=(
            P(SEQ, BLK),
            P(None, BLK + SEQ, None),
            P(None, None, BLK),
            P(None, BLK),
        ),
        check_vma=False,
    )
```

```python
import math

import jax
import jax.numpy as jnp
from jax import lax
from jax.experimental import pallas as pl
from jax.experimental.pallas import tpu as pltpu
from jax.sharding import Mesh, PartitionSpec as P

BASE_DILATION = 4

SEQ = ("y", "zl", "x")
BLK = ("zh", "core")
NEAR = ("zl", "x")
STEPS = (0, 1, 3, 2)

mask_token = 4
gelu_scale = 0.7978845608028654
gelu_cubic = 0.044715
LANES = 256
BF16 = jnp.bfloat16
F32 = jnp.float32

ROWS = 512
TAPS = 9
VOCAB = 5
LOW_GAP, HIGH_GAP = BASE_DILATION, 2 * BASE_DILATION
LOW_REACH, HIGH_REACH = 4 * LOW_GAP, 4 * HIGH_GAP
EDGE = HIGH_REACH
MESSAGE = EDGE + 16
CHUNK = 64
LOWER_COST = 10000000000
PAIRED = (((1,), (1,)), ((), ()))


def gelu_pair(pre_act):
    square = pre_act * pre_act
    tangent = jnp.tanh(gelu_scale * (pre_act + gelu_cubic * square * pre_act))
    half = 0.5 * (1.0 + tangent)
    derivative = half + 0.5 * pre_act * (1.0 - tangent * tangent) * gelu_scale * (
        1.0 + 3.0 * gelu_cubic * square
    )
    return (pre_act * half, derivative)


def call(kernel, outs, scratch, in_specs, *operands, out_specs=None, cost=None):
    extra = {} if in_specs is None else {"in_specs": in_specs, "grid": (1,)}
    if cost is not None:
        extra["cost_estimate"] = pl.CostEstimate(
            flops=cost, transcendentals=0, bytes_accessed=0
        )
    if out_specs is not None:
        extra["out_specs"] = out_specs
    return pl.pallas_call(
        kernel,
        out_shape=outs,
        scratch_shapes=scratch,
        compiler_params=pltpu.CompilerParams(vmem_limit_bytes=16 << 20),
        **extra,
    )(*operands)


def call_staged(kernel, outs, scratch, place, *operands):
    count = len(operands)
    lead = 0 if place is None else 1

    def staged(*refs):
        head, sources, rest = refs[:lead], refs[lead : lead + count], refs[lead + count :]
        held, sems = rest[-count - 1 : -1], rest[-1]
        loads = [
            pltpu.make_async_copy(sources[index], held[index], sems.at[index])
            for index in range(count)
        ]
        for load in loads:
            load.start()
        for load in loads:
            load.wait()
        kernel(*head, *held, *rest[: -count - 1])

    smem = pl.BlockSpec(memory_space=pltpu.SMEM)
    hbm = pl.BlockSpec(memory_space=pltpu.HBM)
    operands = [pltpu.with_memory_space_constraint(cells, pltpu.HBM) for cells in operands]
    return pl.pallas_call(
        staged,
        out_shape=outs,
        in_specs=[smem] * lead + [hbm] * count,
        scratch_shapes=list(scratch)
        + [pltpu.VMEM(cells.shape, cells.dtype) for cells in operands]
        + [pltpu.SemaphoreType.DMA((count,))],
        compiler_params=pltpu.CompilerParams(vmem_limit_bytes=24 << 20),
    )(*(() if place is None else (place,)), *operands)


def shape(dims, kind):
    return jax.ShapeDtypeStruct(dims, kind)


def pack_kernel(saved, ids, next_out, prev_out):
    for out, begin, row in ((next_out, ROWS - EDGE, 3), (prev_out, 0, 0)):
        out[:EDGE] = saved[begin : begin + EDGE]
        line = jnp.broadcast_to(ids[row : row + 1].astype(F32), (MESSAGE - EDGE, 128))
        out[EDGE:] = jnp.concatenate([line, line], axis=1).astype(BF16)


def prep_kernel(
    place, before, after, saved, cot, ids, start, length, embedding, conv,
    slope_up, act_up, slope_low, act_low, masked, hot_out,
    cover, idw, wide, first, table, act_all,
):
    base = place[0] * ROWS - CHUNK
    total = place[1]

    def cover_chunk(index, carry):
        row0 = pl.multiple_of(index * CHUNK, CHUNK)
        here = lax.broadcasted_iota(jnp.int32, (CHUNK, 128), 0) + (base + row0)
        hit = jnp.zeros((CHUNK, 128), jnp.int32)
        for group in range(start.shape[0]):
            gap = here - start[group : group + 1]
            hit = jnp.where((gap >= 0) & (gap < length[group : group + 1]), 1, hit)
        seen = jnp.max(hit, axis=1, keepdims=True).astype(F32)
        cover[pl.ds(row0, CHUNK), :] = jnp.broadcast_to(seen, (CHUNK, 128))
        return carry

    lax.fori_loop(0, ROWS // CHUNK + 2, cover_chunk, 0)

    def column(row):
        return jnp.transpose(jnp.broadcast_to(row.astype(F32), (128, 128)))

    idw[:LOW_REACH] = column(before[EDGE : EDGE + 1, :128])[128 - LOW_REACH :]
    for piece in range(ROWS // 128):
        idw[LOW_REACH + 128 * piece : LOW_REACH + 128 * (piece + 1)] = column(ids[piece : piece + 1])
    idw[LOW_REACH + ROWS :] = column(after[EDGE : EDGE + 1, :128])[:LOW_REACH]
    spread = ROWS + 2 * LOW_REACH
    spot = lax.broadcasted_iota(jnp.int32, (spread, 128), 0) + (base + CHUNK - LOW_REACH)
    lane = lax.broadcasted_iota(jnp.int32, (1, 128), 1)
    tokens = jnp.where(
        cover[CHUNK - LOW_REACH : CHUNK - LOW_REACH + spread] > 0.0,
        float(mask_token),
        idw[...],
    )
    tokens = jnp.where((spot >= 0) & (spot < total), tokens, 7.0)
    idw[...] = tokens
    table[...] = jnp.zeros_like(table)
    table[:VOCAB] = embedding[...].astype(F32)
    hot = jnp.where(tokens == lane.astype(F32), 1.0, 0.0).astype(BF16)
    first[...] = jnp.dot(hot, table[...].astype(BF16), preferred_element_type=F32)

    channel = lax.broadcasted_iota(jnp.int32, (LANES, LANES), 1)
    target = lax.broadcasted_iota(jnp.int32, (LANES, LANES), 0)
    tail = ((channel >> 5) << 2) | (channel & 3)
    low_place = (((channel >> 2) & 7) << 5) | tail
    low_shuffle = jnp.where(low_place == target, 1.0, 0.0).astype(BF16)

    taps_low = [conv[0, index : index + 1].astype(F32) for index in range(TAPS)]
    for chunk in range(ROWS // CHUNK):
        row0 = chunk * CHUNK
        pre = None
        for index in range(TAPS):
            begin = row0 + index * LOW_GAP
            term = taps_low[index] * first[begin : begin + CHUNK]
            pre = term if pre is None else pre + term
        act, slope = gelu_pair(pre)
        slope_low[row0 : row0 + CHUNK] = slope
        act_all[row0 : row0 + CHUNK] = act.astype(BF16)
    act_low[...] = lax.dot_general(
        low_shuffle, act_all[:ROWS], PAIRED, preferred_element_type=F32
    ).astype(BF16)

    picked = idw[:ROWS]
    for index in range(1, TAPS):
        picked = jnp.where((lane >> 3) == index, idw[index * LOW_GAP : index * LOW_GAP + ROWS], picked)
    kind = lane & 7
    live = (kind < VOCAB) & (lane < 8 * TAPS)
    hot = jnp.where((picked == kind.astype(F32)) & live, 1.0, 0.0)
    hot_out[...] = jnp.transpose(hot).astype(BF16)

    wide[:HIGH_REACH] = before[:HIGH_REACH].astype(F32)
    wide[HIGH_REACH : HIGH_REACH + ROWS] = saved[...].astype(F32)
    wide[HIGH_REACH + ROWS :] = after[:HIGH_REACH].astype(F32)
    taps_up = [conv[1, index : index + 1].astype(F32) for index in range(TAPS)]
    for chunk in range(ROWS // CHUNK):
        row0 = chunk * CHUNK
        pre = None
        for index in range(TAPS):
            begin = row0 + index * HIGH_GAP
            term = taps_up[index] * wide[begin : begin + CHUNK]
            pre = term if pre is None else pre + term
        act, slope = gelu_pair(pre)
        seen = cover[CHUNK + row0 : 2 * CHUNK + row0] > 0.0
        seen = jnp.concatenate([seen, seen], axis=1)
        slope_up[row0 : row0 + CHUNK] = jnp.where(seen, slope, 0.0)
        act_all[row0 : row0 + CHUNK] = jnp.where(seen, act, 0.0).astype(BF16)
        masked[row0 : row0 + CHUNK] = jnp.where(
            seen, cot[row0 : row0 + CHUNK].astype(F32), 0.0
        ).astype(BF16)
    act_up[...] = lax.dot_general(
        low_shuffle, act_all[:ROWS], PAIRED, preferred_element_type=F32
    ).astype(BF16)


def chip_block(place, step):
    return (place[2] - step) & 3


def weight_columns(weights, place, step, core):
    block = chip_block(place, step) * 2 + core
    return weights[0, :, pl.ds(pl.multiple_of(block * LANES, LANES), LANES)]


def product_over_blocks(place, mine, pairs, weights):
    total = None
    for index, step in enumerate(STEPS):
        term = lax.dot_general(
            mine[index][...], weight_columns(weights, place, step, place[3]), PAIRED,
            preferred_element_type=F32,
        )
        total = term if total is None else total + term
    for index, step in enumerate(STEPS):
        total = total + lax.dot_general(
            pairs[index // 2][index % 2], weight_columns(weights, place, step, 1 - place[3]),
            PAIRED, preferred_element_type=F32,
        )
    return total


def upper_kernel(place, m0, m1, m2, m3, p0, p1, weights, slope, grad_out, head_out, tail_out):
    grad = product_over_blocks(place, (m0, m1, m2, m3), (p0, p1), weights) * slope[...]
    grad = grad.astype(BF16)
    grad_out[...] = grad
    head_out[...] = grad[:HIGH_REACH]
    tail_out[...] = grad[ROWS - HIGH_REACH :]


def outer_product(act, mine, pairs, out, stage, sems):
    copies = []
    for index in range(2 * len(STEPS)):
        half = index % len(STEPS)
        piece = mine[half][...] if index < len(STEPS) else pairs[half // 2][half % 2]
        lanes = slice(index * LANES, (index + 1) * LANES)
        stage[:, lanes] = jnp.dot(act[...], piece, preferred_element_type=F32).astype(BF16)
        copies.append(
            pltpu.make_async_copy(stage.at[:, lanes], out.at[:, lanes], sems.at[index])
        )
        copies[-1].start()
    return copies


def upper_outer_kernel(
    act, m0, m1, m2, m3, p0, p1, grad, before, saved, after, out, tap_out, wide, stage, sems
):
    copies = outer_product(act, (m0, m1, m2, m3), (p0, p1), out, stage, sems)
    wide[:HIGH_REACH] = before[:HIGH_REACH].astype(F32)
    wide[HIGH_REACH : HIGH_REACH + ROWS] = saved[...].astype(F32)
    wide[HIGH_REACH + ROWS :] = after[:HIGH_REACH].astype(F32)
    sums = [jnp.zeros((8, LANES), F32) for index in range(TAPS)]
    for chunk in range(ROWS // CHUNK):
        row0 = chunk * CHUNK
        grad_wide = grad[row0 : row0 + CHUNK].astype(F32)
        for index in range(TAPS):
            begin = row0 + index * HIGH_GAP
            term = grad_wide * wide[begin : begin + CHUNK]
            sums[index] = sums[index] + jnp.sum(term.reshape(CHUNK // 8, 8, LANES), axis=0)
    tap_out[...] = jnp.zeros_like(tap_out)
    for index in range(TAPS):
        tap_out[index : index + 1] = jnp.sum(sums[index], axis=0, keepdims=True)
    for copy in copies:
        copy.wait()


def lower_kernel(
    place, act, m0, m1, m2, m3, p0, p1, weights, slope, hot, up_row, embedding, conv, upper_taps,
    out, grad_out, small, table, stage, sems,
):
    mine, pairs = (m0, m1, m2, m3), (p0, p1)
    grad = (product_over_blocks(place, mine, pairs, weights) * slope[...]).astype(BF16)
    grad_out[...] = grad
    copies = outer_product(act, mine, pairs, out, stage, sems)
    picked = jnp.dot(hot[...], grad, preferred_element_type=F32)
    embed = jnp.dot(hot[32:48], up_row[...], preferred_element_type=F32)[:8]
    table[...] = jnp.zeros_like(table)
    table[:VOCAB] = embedding[...].astype(F32)
    small[...] = jnp.zeros_like(small)
    for index in range(TAPS):
        piece = picked[index * 8 : index * 8 + 8]
        small[index : index + 1] = jnp.sum(piece * table[...], axis=0, keepdims=True)
        embed = embed + piece * conv[0, index : index + 1].astype(F32)
    small[TAPS : TAPS + VOCAB] = embed[:VOCAB]
    small[TAPS + VOCAB : 2 * TAPS + VOCAB] = upper_taps[:TAPS]
    packed = small[...].astype(BF16)
    for index in range(LANES // 32):
        stage[index * 32 : (index + 1) * 32, 8 * LANES :] = packed
    last = pltpu.make_async_copy(
        stage.at[:, 8 * LANES :], out.at[:, 8 * LANES :], sems.at[8]
    )
    last.start()
    for copy in copies + [last]:
        copy.wait()


def add_up(pieces):
    running = pieces[0].astype(F32)
    for index in range(1, pieces.shape[0]):
        running = running + pieces[index].astype(F32)
    return running


def upper_sum_kernel(pieces, out):
    out[...] = add_up(pieces).astype(BF16)


def middle_kernel(pieces, upper, out):
    running = pieces[0].astype(F32)
    for index in range(1, pieces.shape[0]):
        running = running + pieces[index].astype(F32)
    width = 8 * LANES
    upper = upper[...]
    small = running[:, width:].astype(BF16)
    lower = running[:, :width].astype(BF16)
    for far in range(8):
        out[far, :, :width] = lower[4 * far : 4 * far + 4]
        out[far, :, width : 2 * width] = upper[4 * far : 4 * far + 4]
        for group in range(6):
            begin = 2 * width + group * LANES
            out[far, :, begin : begin + LANES] = small[4 * group : 4 * group + 4]


def final_kernel(place, pieces, weight_out, kernel_out, embed_out, *, scale):
    running = pieces[0].astype(F32)
    for index in range(1, pieces.shape[0]):
        running = running + pieces[index].astype(F32)
    running = running * scale
    width = 8 * LANES
    for index in range(8):
        step = STEPS[index % 4]
        core = place[3] if index < 4 else 1 - place[3]
        spot = pl.multiple_of((chip_block(place, step) * 2 + core) * LANES, LANES)
        for layer in range(2):
            begin = layer * width + index * LANES
            weight_out[layer, :, pl.ds(spot, LANES)] = running[:, begin : begin + LANES]

    def small_row(row):
        begin = 2 * width + (row // 4) * LANES
        return running[row % 4 : row % 4 + 1, begin : begin + LANES]

    for index in range(TAPS):
        kernel_out[index, 0:1] = small_row(index)
        kernel_out[index, 1:2] = small_row(TAPS + VOCAB + index)
    for index in range(VOCAB):
        embed_out[index : index + 1] = small_row(TAPS + index)


def spread_kernel(base, grad, before, after, conv, out, wide, *, layer, gap):
    reach = gap * (TAPS // 2)
    wide[:reach] = before[...].astype(F32)
    wide[reach : reach + ROWS] = grad[...].astype(F32)
    wide[reach + ROWS :] = after[...].astype(F32)
    for chunk in range(ROWS // CHUNK):
        row0 = chunk * CHUNK
        running = base[row0 : row0 + CHUNK].astype(F32)
        for index in range(TAPS):
            begin = row0 + (TAPS - 1 - index) * gap
            tap = conv[layer, index : index + 1].astype(F32)
            running = running + tap * wide[begin : begin + CHUNK]
        out[row0 : row0 + CHUNK] = running.astype(BF16)


def spread(base, grad, before, after, conv, layer, gap):
    def kernel(*refs):
        spread_kernel(*refs, layer=layer, gap=gap)

    scratch = [pltpu.VMEM((ROWS + gap * (TAPS - 1), LANES), F32)]
    out = shape((ROWS, LANES), BF16)
    return call(kernel, out, scratch, None, base, grad, before, after, conv)


def seq_shift(cells, step):
    count = lax.axis_size(SEQ)
    if step > 0:
        return lax.ppermute(cells, SEQ, [(i, i + 1) for i in range(count - 1)])
    return lax.ppermute(cells, SEQ, [(i + 1, i) for i in range(count - 1)])


def ring_copies(slab):
    count = lax.axis_size("zh")
    moved = {0: slab}
    for step in (2, 1, 3):
        moved[step] = lax.ppermute(slab, "zh", [(i, (i + step) % count) for i in range(count)])
    return [moved[step] for step in STEPS]


def core_swap(cells):
    return lax.ppermute(cells, "core", [(0, 1), (1, 0)])


def swapped_pairs(mine):
    return core_swap(jnp.stack(mine[:2])), core_swap(jnp.stack(mine[2:]))


def on_device(
    base_ids, span_start, span_length, embedding, conv_kernel, mix_weight, saved_input, cotangent
):
    total_rows = ROWS * lax.axis_size(SEQ)
    place = jnp.stack(
        [
            lax.axis_index(SEQ),
            jnp.int32(total_rows),
            lax.axis_index("zh"),
            lax.axis_index("core"),
            lax.axis_index("zl"),
        ]
    ).astype(jnp.int32)
    smem = pl.BlockSpec(memory_space=pltpu.SMEM)
    vmem = pl.BlockSpec(memory_space=pltpu.VMEM)
    ids = base_ids.reshape(ROWS // 128, 128)
    slab = shape((ROWS, LANES), BF16)
    slab_wide = shape((ROWS, LANES), F32)
    turned = shape((LANES, ROWS), BF16)

    message = shape((MESSAGE, LANES), BF16)
    to_next, to_prev = call_staged(
        pack_kernel, (message, message), [], None, saved_input, ids
    )
    before = seq_shift(to_next, 1)
    after = seq_shift(to_prev, -1)
    mine = ring_copies(cotangent)

    slope_up, act_up, slope_low, act_low, masked, hot = call_staged(
        prep_kernel,
        (slab_wide, turned, slab_wide, turned, slab, shape((128, ROWS), BF16)),
        [
            pltpu.VMEM((ROWS + 2 * CHUNK, 128), F32),
            pltpu.VMEM((ROWS + 2 * LOW_REACH, 128), F32),
            pltpu.VMEM((ROWS + 2 * HIGH_REACH, LANES), F32),
            pltpu.VMEM((ROWS + 2 * LOW_REACH, LANES), F32),
            pltpu.VMEM((128, LANES), F32),
            pltpu.VMEM((ROWS, LANES), BF16),
        ],
        place, before, after, saved_input, cotangent, ids,
        span_start.reshape(-1, 128), span_length.reshape(-1, 128), embedding, conv_kernel,
    )
    slope_up, mine[1], mine[2], mine[3] = lax.optimization_barrier(
        (slope_up, mine[1], mine[2], mine[3])
    )
    pairs = swapped_pairs(mine)

    weight_specs = [
        pl.BlockSpec((1, LANES, 8 * LANES), lambda step: (0, 0, 0)),
        pl.BlockSpec((1, LANES, 8 * LANES), lambda step: (1, 0, 0)),
    ]
    rim = shape((HIGH_REACH, LANES), BF16)
    grad_upper, head, tail = call(
        upper_kernel,
        (slab, rim, rim),
        [],
        [smem] + [vmem] * 6 + [weight_specs[1], vmem],
        place, *mine, *pairs, mix_weight, slope_up,
    )
    up_before = seq_shift(tail, 1)
    up_after = seq_shift(head, -1)
    up_mid = spread(masked, grad_upper, up_before, up_after, conv_kernel, 1, HIGH_GAP)
    mid = ring_copies(up_mid)
    mid_pairs = swapped_pairs(mid)

    far_specs = (pl.BlockSpec(memory_space=pltpu.HBM), vmem)
    upper_outer, upper_taps = call(
        upper_outer_kernel,
        (pltpu.HBM((LANES, 8 * LANES), BF16), shape((16, LANES), F32)),
        [
            pltpu.VMEM((ROWS + 2 * HIGH_REACH, LANES), F32),
            pltpu.VMEM((LANES, 8 * LANES), BF16),
            pltpu.SemaphoreType.DMA((8,)),
        ],
        [vmem] * 11,
        act_up, *mine, *pairs, grad_upper, before, saved_input, after, out_specs=far_specs,
    )
    pieces = lax.all_to_all(upper_outer.reshape(8, 32, 8 * LANES), NEAR, 0, 0)
    upper_sum = call(upper_sum_kernel, shape((32, 8 * LANES), BF16), [], None, pieces)

    lower_outer, grad_lower = call(
        lower_kernel,
        (pltpu.HBM((LANES, 9 * LANES), BF16), slab),
        [
            pltpu.VMEM((32, LANES), F32),
            pltpu.VMEM((8, LANES), F32),
            pltpu.VMEM((LANES, 9 * LANES), BF16),
            pltpu.SemaphoreType.DMA((9,)),
        ],
        [smem] + [vmem] * 7 + [weight_specs[0]] + [vmem] * 6,
        place, act_low, *mid, *mid_pairs, mix_weight, slope_low, hot, up_mid, embedding,
        conv_kernel, upper_taps, out_specs=far_specs, cost=LOWER_COST,
    )
    low_before = seq_shift(grad_lower[ROWS - LOW_REACH :], 1)
    low_after = seq_shift(grad_lower[:LOW_REACH], -1)
    lower_outer, low_before, low_after = lax.optimization_barrier(
        (lower_outer, low_before, low_after)
    )
    pieces = lax.all_to_all(lower_outer.reshape(8, 32, 9 * LANES), NEAR, 0, 0)
    input_grad = spread(up_mid, grad_lower, low_before, low_after, conv_kernel, 0, LOW_GAP)
    pieces, input_grad = lax.optimization_barrier((pieces, input_grad))
    middle = call(
        middle_kernel, shape((8, 4, 22 * LANES), BF16), [], None, pieces, upper_sum
    )
    pieces = lax.all_to_all(middle, "y", 0, 0)

    def finish(*refs):
        final_kernel(*refs, scale=1.0 / math.sqrt(total_rows))

    weight_grad, kernel_grad, embed_grad = call(
        finish,
        (shape((2, 4, 8 * LANES), F32), shape((TAPS, 2, LANES), F32), shape((VOCAB, LANES), F32)),
        [],
        [smem, vmem],
        place, pieces,
    )
    return (input_grad, weight_grad, kernel_grad.transpose(1, 0, 2), embed_grad)


def solution(mesh):
    fine = Mesh(mesh.devices.reshape(8, 2, 4, 4, 2), SEQ + BLK)
    placed = (
        P(SEQ),
        P(),
        P(),
        P(None, BLK),
        P(None, None, BLK),
        P(None, BLK, None),
        P(SEQ, BLK),
        P(SEQ, BLK),
    )
    return jax.shard_map(
        on_device,
        mesh=fine,
        in_specs=placed,
        out_specs=(
            P(SEQ, BLK),
            P(None, BLK + SEQ, None),
            P(None, None, BLK),
            P(None, BLK),
        ),
        check_vma=False,
    )
```
